32 devices in a mesh: groups: 2 (over y), date: 4 (over x, core), col: 4 (over z).
Axes of the slice: x: 2, y: 2, z: 4, core: 2. Of those that a mesh axis runs over, the one named last changes fastest.
Arguments:
- scenes: bfloat16 [16, 2, 128, 1024], P('date', None, 'groups', 'col'), parts along dimension 2, may hold values from -6 to 6
- pair_dates: int32 [96, 2], P('date'), may hold values from 0 to 15, as said below
- pair_count: int32 [4], P('date'), may hold values from 12 to 24, as said below
- inverse: float32 [15, 96], replicated, may hold values from -0.625 to 0.625
Outputs:
- series: float32 [15, 2, 64, 128], P(None, None, ('groups', 'date'), 'col'), parts along dimension 2
The draws below stay inside these ranges and needn't reach their ends.
There are 2 independent parts, one for each index of `groups`. The reference program is written for one: setup_inputs(seed, part) draws one part's arguments, and reference() takes and returns one part's arrays. A program takes and returns all parts, laid end to end along the dimension named above; an argument that names none is the same for every part. Nothing has to cross between parts.
Inputs may be any that keep to these rules, and one draw needn't show every extreme that they name: `pair_dates`: each row names a reference acquisition and a later secondary one. Slots i * 24 to (i + 1) * 24 - 1 belong to owner i (index i of date); every slot of owner i names acquisitions held by indices i - 2 to i + 2 of date (as far as these exist), and one live pair of every owner names the lowest and the highest acquisition of that range. `pair_count`: entry i is the number of live slots of owner i; they come first in its block and the other slots are ignored. Some owner has all its slots live.
All inputs are finite; a program needn't handle non-finite values.
Results may differ from the reference program's by a relative error of at most 0.0003.
Values may be sent and summed in bfloat16 or wider, within the bound.
A program may use at most 64 MiB of HBM per device.

```python
import jax
import jax.numpy as jnp
from jax import lax

DATE_DEV = 4
PAIR_DEV = 24
HOPS = 2
ROWS = 64
DATES = 16
PAIRS = 96
NPAR = 15
COLS = 1024
MLR = 32
MLC = 128


def draw_pair_dates(key, part):
    indices = jnp.arange(PAIRS, dtype=jnp.int32)
    owners = indices // PAIR_DEV
    within = indices % PAIR_DEV
    lowest = jnp.maximum(0, (owners - HOPS) * DATE_DEV)
    highest = jnp.minimum(DATES, (owners + HOPS + 1) * DATE_DEV)
    key_first, key_step = jax.random.split(jax.random.fold_in(key, 11))
    leading = jax.random.randint(key_first, (PAIRS,), lowest, highest - 1)
    stepping = jax.random.randint(key_step, (PAIRS,), 1, 7)
    trailing = jnp.minimum(leading + stepping, highest - 1)
    leading = jnp.where(within == 0, lowest, leading)
    trailing = jnp.where(within == 0, jnp.minimum(lowest + stepping, highest - 1), trailing)
    leading = jnp.where(within == 1, jnp.maximum(lowest, highest - 1 - stepping), leading)
    trailing = jnp.where(within == 1, highest - 1, trailing)
    leading = jnp.where(within == 2, lowest, leading)
    trailing = jnp.where(within == 2, highest - 1, trailing)
    return jnp.stack([leading, trailing], axis=1).astype(jnp.int32)


def draw_pair_count(key, part):
    owner_total = PAIRS // PAIR_DEV
    key_counts, key_full = jax.random.split(jax.random.fold_in(key, 23))
    counts = jax.random.randint(key_counts, (owner_total,), PAIR_DEV // 2, PAIR_DEV + 1)
    busiest = jax.random.randint(key_full, (), 0, owner_total)
    return jnp.where(jnp.arange(owner_total) == busiest, PAIR_DEV, counts).astype(jnp.int32)


def shard_levels(stream_key, dims, cuts, smallest, largest):
    def one(dim, blocks):
        heights = jax.random.uniform(jax.random.fold_in(jax.random.fold_in(stream_key, 6), dim), (blocks,), jnp.float32, smallest / len(cuts), largest / len(cuts))
        return jnp.repeat(jnp.exp(heights), dims[dim] // blocks).reshape((-1,) + (1,) * (len(dims) - dim - 1))

    factor_of = one(*cuts[0])
    for cut in cuts[1:]:
        factor_of = factor_of * one(*cut)
    return factor_of


def noise(own_key, dims, spread, reach, pieces=(), kind=jnp.bfloat16):
    array = spread * jax.random.normal(own_key, dims, jnp.float32)
    if pieces:
        array = array * shard_levels(own_key, dims, pieces, -0.22, 0.18)
    return jnp.clip(array, -reach, reach).astype(kind)


def setup_inputs(seed: int = 0, part: int = 0) -> dict:
    seeds = jax.random.split(jax.random.key(seed), 5)
    part_keys = jax.random.split(jax.random.fold_in(seeds[4], part), 5)
    return {
        "scenes": noise(part_keys[0], (DATES, 2, ROWS, COLS), 1.0, 6.0, ((0, 4), (3, 4))),
        "pair_dates": draw_pair_dates(jax.random.fold_in(seeds[4], 71), part),
        "pair_count": draw_pair_count(jax.random.fold_in(seeds[4], 71), part),
        "inverse": noise(seeds[3], (NPAR, PAIRS), PAIRS ** -0.5, 0.625, (), jnp.float32),
    }


def look_weights():
    offsets = jnp.arange(16).astype(jnp.float32)
    return (8.0 - jnp.abs(offsets - 7.5)) / 64.0


def reference(scenes, pair_dates, pair_count, inverse):
    indices = jnp.arange(PAIRS).astype(jnp.int32)
    owners = indices // PAIR_DEV
    within = indices % PAIR_DEV
    living = (within < pair_count[owners]).astype(jnp.float32)
    weights = look_weights()

    def one_pair(member):
        pair_row, alive = member
        primary = scenes[pair_row[0]].astype(jnp.float32)
        secondary = scenes[pair_row[1]].astype(jnp.float32)
        real_part = primary[0] * secondary[0] + primary[1] * secondary[1]
        imaginary = primary[1] * secondary[0] - primary[0] * secondary[1]
        products = jnp.stack([real_part, imaginary]) * alive
        halved = 0.5 * (products[:, 0::2, :] + products[:, 1::2, :])
        padded = jnp.pad(halved, ((0, 0), (0, 0), (4, 4)))
        looked = jnp.zeros((2, MLR, MLC), jnp.float32)
        for offset in range(16):
            looked = looked + weights[offset] * padded[:, :, offset: offset + COLS: 8]
        return looked

    multilooked = lax.map(one_pair, (pair_dates, living))
    flattened = multilooked.reshape(PAIRS, 2 * MLR * MLC)
    series = jnp.dot(inverse, flattened, precision=lax.Precision.HIGHEST, preferred_element_type=jnp.float32)
    return series.reshape(NPAR, 2, MLR, MLC)
```

```python
import functools

import jax
import jax.numpy as jnp
from jax import lax
from jax.experimental import pallas as pl
from jax.experimental.pallas import tpu as pltpu
from jax.sharding import PartitionSpec as P

MESH = pl.DeviceIdType.MESH
F32 = jnp.float32
BF16 = jnp.bfloat16
EDGE = 4


def flipped(place, slot):
    bit = 1
    out = place
    while bit <= slot:
        if slot & bit:
            out = out + bit - 2 * bit * ((place // bit) % 2)
        bit *= 2
    return out


def split(value):
    high = value.astype(BF16)
    return high, (value - high.astype(F32)).astype(BF16)


def iota(shape, dim):
    return lax.broadcasted_iota(jnp.int32, shape, dim)


def stack_kernel(
    cfg,
    scenes, dates, count, inverse, out,
    local, base, dates_in, counts_in, edge_out, edge_in,
    raw, cells, h_high, h_low, weights, k_high, k_low, l_high, l_low,
    load_sem, send_sem, recv_sem, dates_send, dates_recv, count_send, count_recv, edge_send, edge_recv,
):
    D, C, A, R, X, S, NP = (cfg[k] for k in ("D", "C", "A", "R", "X", "S", "NP"))
    dates_total = D * A
    T = X // 128
    TT = T + 1
    half = R // 2
    looks = X // 8
    block = A * A * half
    diag = block // 2
    date = lax.axis_index("date")
    col = lax.axis_index("col")
    has_left = col > 0
    has_right = col < C - 1

    load = pltpu.make_async_copy(scenes, local, load_sem)
    load.start()

    barrier = pltpu.get_barrier_semaphore()
    for r in range(1, D):
        pl.semaphore_signal(barrier, inc=1, device_id={"date": flipped(date, r)}, device_id_type=MESH)

    @pl.when(has_left)
    def _():
        for r in range(D):
            pl.semaphore_signal(barrier, inc=1, device_id={"date": flipped(date, r), "col": col - 1}, device_id_type=MESH)

    @pl.when(has_right)
    def _():
        for r in range(D):
            pl.semaphore_signal(barrier, inc=1, device_id={"date": flipped(date, r), "col": col + 1}, device_id_type=MESH)

    load.wait()
    lane = iota((D * R, 128), 1)
    to_left = jnp.zeros((D * R, 128), F32)
    to_right = jnp.zeros((D * R, 128), F32)
    for i in range(2 * A):
        first = local[i // 2, i % 2, :, 0:128].astype(F32)
        last = local[i // 2, i % 2, :, X - 128:X].astype(F32)
        shift = (8 * i + EDGE) % 128
        to_left = jnp.where(lane // EDGE == 2 * i + 1, pltpu.roll(first, shift, 1), to_left)
        shift = (8 * i + EDGE) % 128
        to_right = jnp.where(lane // EDGE == 2 * i, pltpu.roll(last, shift, 1), to_right)
    edge_out[0] = to_right.astype(BF16)
    edge_out[1] = to_left.astype(BF16)

    @pl.when(jnp.logical_not(has_left))
    def _():
        edge_in[0] = jnp.zeros((D, R, 128), BF16)

    @pl.when(jnp.logical_not(has_right))
    def _():
        edge_in[1] = jnp.zeros((D, R, 128), BF16)

    pl.semaphore_wait(barrier, D - 1 + D * (has_left.astype(jnp.int32) + has_right.astype(jnp.int32)))

    def rows_of(place):
        return pl.ds(pl.multiple_of(place * R, R), R)

    def remote(src, dst, ssem, rsem, device):
        return pltpu.make_async_remote_copy(src_ref=src, dst_ref=dst, send_sem=ssem, recv_sem=rsem, device_id=device, device_id_type=MESH)

    to_next = {}
    order = list(range(D - 1, 0, -1))
    for r in range(1, D):
        there = flipped(date, r)
        to_next["dates", r] = remote(dates, dates_in.at[date], dates_send.at[r], dates_recv.at[r], {"date": there})
        to_next["count", r] = remote(count, counts_in.at[date], count_send.at[r], count_recv.at[r], {"date": there})
        to_next["scene", r] = remote(scenes.at[:, :, rows_of(there), :], base.at[r], send_sem.at[r], recv_sem.at[r], {"date": there})
    for r in range(D):
        there = flipped(date, r)
        to_next["right", r] = remote(edge_out.at[0, rows_of(there)], edge_in.at[0, r], edge_send.at[0, r], edge_recv.at[0, r], {"date": there, "col": col + 1})
        to_next["left", r] = remote(edge_out.at[1, rows_of(there)], edge_in.at[1, r], edge_send.at[1, r], edge_recv.at[1, r], {"date": there, "col": col - 1})
    for r in order:
        to_next["dates", r].start()
        to_next["count", r].start()

    @pl.when(has_right)
    def _():
        for r in order + [0]:
            to_next["right", r].start()

    @pl.when(has_left)
    def _():
        for r in order + [0]:
            to_next["left", r].start()

    for r in cfg["send_order"]:
        to_next["scene", r].start()

    dates_in[date] = dates[...]
    counts_in[date] = count[...]

    row = iota((TT * 128, 128), 0)
    spot = row - TT * 128 + 128
    column = jnp.where(spot < 0, row, jnp.where(spot < EDGE, spot - EDGE, spot - EDGE + X))
    usable = (spot < 2 * EDGE)
    target = iota((TT * 128, 128), 1)
    for c in range(2):
        look = target - 64 * c
        offset = column - 8 * look + 4
        inside = usable & (look >= 0) & (look < looks) & (offset >= 0) & (offset < 16)
        value = jnp.where(inside, (8.0 - jnp.abs(offset.astype(F32) - 7.5)) / 128.0, 0.0)
        weights[c * TT * 128:(c + 1) * TT * 128, :] = value.astype(BF16)

    def unpack(slot, main):
        for c in range(2):
            for t in range(T):
                for i in range(A):
                    at = ((c * TT + t) * A + i) * R
                    raw[at:at + R, :] = main(i, c)[:, t * 128:(t + 1) * 128].astype(F32)
        edges = edge_in[0, slot].astype(F32) + edge_in[1, slot].astype(F32)
        for c in range(2):
            for i in range(A):
                at = ((c * TT + T) * A + i) * R
                shift = (128 - 8 * (2 * i + c)) % 128
                raw[at:at + R, :] = pltpu.roll(edges, shift, 1) if shift else edges
        total = 2 * TT * A * half
        for parity in range(2):
            got = raw[pl.ds(parity, total, stride=2), :]
            cells[parity, :, slot * A:(slot + 1) * A] = got.reshape(2 * TT, A, half, 128)

    def emit(at, pieces):
        rows = pieces[0][0].shape[0]
        for t, both in enumerate(pieces):
            for c in range(2):
                high, low = split(both[c])
                h_high[at:at + rows, (c * TT + t) * 128:(c * TT + t + 1) * 128] = high
                h_low[at:at + rows, (c * TT + t) * 128:(c * TT + t + 1) * 128] = low

    def product(p_of, s_of, t):
        real = imaginary = None
        for parity in range(2):
            p0, p1 = p_of(parity, t), p_of(parity, TT + t)
            s0, s1 = s_of(parity, t), s_of(parity, TT + t)
            one = p0 * s0 + p1 * s1
            two = p1 * s0 - p0 * s1
            real = one if real is None else real + one
            imaginary = two if imaginary is None else imaginary + two
        return real, imaginary

    def pair_order(ra, rb):
        bit = 1
        while 2 * bit <= (ra ^ rb):
            bit *= 2
        swap = (flipped(date, ra) // bit) % 2
        low = ra + swap * (rb - ra)
        high = rb - swap * (rb - ra)
        return low, high

    chunks = []

    def cross(ra, rb):
        at = len(chunks) * block
        chunks.append((ra, rb))
        low, high = pair_order(ra, rb)
        for i in range(A):
            pieces = []
            for t in range(TT):
                both = product(
                    lambda q, n: cells[q, n, low * A + i][None],
                    lambda q, n: cells[q, n, pl.ds(high * A, A)], t)
                pieces.append([v.reshape(A * half, 128) for v in both])
            emit(at + i * A * half, pieces)

    def within(ra):
        at = len(chunks) * block
        chunks.append((ra, ra + 1))
        for side in range(2):
            slot = ra + side
            pieces = []
            for t in range(TT):
                parts = [], []
                for step in range(1, A):
                    both = product(
                        lambda q, n: cells[q, n, slot * A:slot * A + A - step],
                        lambda q, n: cells[q, n, slot * A + step:slot * A + A], t)
                    for c in range(2):
                        parts[c].append(both[c].reshape((A - step) * half, 128))
                pad = jnp.zeros((diag - A * (A - 1) // 2 * half, 128), F32)
                pieces.append([jnp.concatenate(parts[c] + [pad], axis=0) for c in range(2)])
            emit(at + side * diag, pieces)

    def look(start, stop):
        rows = slice(start * block, stop * block)
        got = jnp.dot(h_high[rows, :], weights[...], preferred_element_type=F32)
        got = got + jnp.dot(h_low[rows, :], weights[...], preferred_element_type=F32)
        l_high[rows, :], l_low[rows, :] = split(got)

    def wait_edges(r):
        @pl.when(has_left)
        def _():
            to_next["right", r].wait_recv()

        @pl.when(has_right)
        def _():
            to_next["left", r].wait_recv()

    wait_edges(0)
    unpack(0, lambda i, c: local[i, c, rows_of(date), :])

    order_in = cfg["order_in"]
    looked = 0
    arrived = [0]
    for r in order_in:
        if r == order_in[0]:
            for q in range(1, D):
                to_next["dates", q].wait_recv()
                to_next["count", q].wait_recv()
        wait_edges(r)
        to_next["scene", r].wait_recv()
        unpack(r, lambda i, c: base[r, i, c])
        if (r ^ 1) in arrived:
            within(r & ~1)
        for other in arrived:
            cross(min(other, r), max(other, r))
        arrived.append(r)
        look(looked, len(chunks))
        looked = len(chunks)
        if r == order_in[0]:
            invert_matrix(cfg, date, dates_in, counts_in, inverse, k_high, k_low, pair_order)

    lh, ll = l_high[...], l_low[...]
    kh = k_high[...]
    series = jnp.dot(kh, lh, preferred_element_type=F32)
    series = series + jnp.dot(kh, ll, preferred_element_type=F32)
    series = series + jnp.dot(k_low[...], lh, preferred_element_type=F32)
    for c in range(2):
        out[:, c] = series[:, c * 64:c * 64 + looks].reshape(NP, half, looks)

    for r in range(1, D):
        for kind in ("dates", "count", "scene"):
            to_next[kind, r].wait_send()

    @pl.when(has_right)
    def _():
        for r in range(D):
            to_next["right", r].wait_send()

    @pl.when(has_left)
    def _():
        for r in range(D):
            to_next["left", r].wait_send()


def chunk_list(order_in):
    chunks, arrived = [], [0]
    for r in order_in:
        if (r ^ 1) in arrived:
            chunks.append((r & ~1, None))
        for other in arrived:
            chunks.append((min(other, r), max(other, r)))
        arrived.append(r)
    return chunks


def invert_matrix(cfg, date, dates_in, counts_in, inverse, k_high, k_low, pair_order):
    D, A, R, S, NP = (cfg[k] for k in ("D", "A", "R", "S", "NP"))
    half = R // 2
    block = A * A * half
    diag = block // 2
    total = D * A
    codes = []
    for d in range(D):
        row = dates_in[d, 0:1, :] * total + dates_in[d, 1:2, :]
        live = iota((1, S), 1) < counts_in[d]
        codes.append(jnp.where(live, row, -1).astype(F32))
    codes.append(jnp.full((8 - D % 8 if D % 8 else 8, S), -1.0, F32))
    table = jnp.concatenate(codes, axis=0)
    table = jnp.concatenate([table, jnp.full((table.shape[0], 128 - S), -1.0, F32)], axis=1)
    turned = jnp.transpose(table)
    code = jnp.concatenate([turned[0:S, d:d + 1] for d in range(D)], axis=0).astype(jnp.int32)
    inv = inverse[...]
    spread = jnp.broadcast_to(inv[:, None, :], (NP, half, D * S)).reshape(NP * half, D * S)
    spread_high, spread_low = split(spread)
    place = iota((1, block), 1)
    same = (iota((NP * half, block), 0) % half) == (iota((NP * half, block), 1) % half)
    for n, (ra, rb) in enumerate(chunk_list(cfg["order_in"])):
        if rb is None:
            slot = place // diag
            index = (place % diag) // half
            first = jnp.zeros_like(place)
            second = jnp.zeros_like(place) - 1
            at = 0
            for step in range(1, A):
                for i in range(A - step):
                    first = jnp.where(index == at, i, first)
                    second = jnp.where(index == at, i + step, second)
                    at += 1
            owner = jnp.where(slot == 0, flipped(date, ra), flipped(date, ra + 1))
            want = jnp.where(second >= 0, (owner * A + first) * total + owner * A + second, -2)
        else:
            low, high = pair_order(ra, rb)
            lo_date, hi_date = cfg["place_of"](date, low), cfg["place_of"](date, high)
            first = lo_date * A + place // (A * half)
            second = hi_date * A + (place // half) % A
            want = first * total + second
        hit = jnp.where(code == want, 1.0, 0.0).astype(BF16)
        value = jnp.dot(spread_high, hit, preferred_element_type=F32) + jnp.dot(spread_low, hit, preferred_element_type=F32)
        value = jnp.where(same, value, 0.0)
        columns = slice(n * block, (n + 1) * block)
        k_high[:, columns], k_low[:, columns] = split(value)


def padded(cells, sides, width):
    for axis, dim in sides:
        count = lax.axis_size(axis)
        ends = count - 1
        head = lax.slice_in_dim(cells, 0, width, axis=dim)
        tail = lax.slice_in_dim(cells, cells.shape[dim] - width, cells.shape[dim], axis=dim)
        cells = jnp.concatenate(
            [
                lax.ppermute(tail, axis, [(i, (i + 1) % count) for i in range(ends)]),
                cells,
                lax.ppermute(head, axis, [((i + 1) % count, i) for i in range(ends)]),
            ],
            axis=dim,
        )
    return cells


def look_matrix(padded_width, looks_here):
    column = jnp.arange(padded_width, dtype=jnp.int32)[:, None]
    target = jnp.arange(looks_here, dtype=jnp.int32)[None, :]
    offset = (column - 8 * target).astype(jnp.float32)
    inside = (offset >= 0.0) & (offset < 16.0)
    return jnp.where(inside, (8.0 - jnp.abs(offset - 7.5)) / 64.0, 0.0)


def plain_device(scenes, pair_dates, pair_count, inverse):
    slot_count = pair_dates.shape[0]
    looks_here = scenes.shape[3] // 8
    base = lax.all_to_all(scenes, "date", split_axis=2, concat_axis=0, tiled=True)
    used_dates, used_counts = (
        lax.all_gather(pair_dates, "date", axis=0, tiled=True),
        lax.all_gather(pair_count, "date", axis=0, tiled=True),
    )
    slot_index = jnp.arange(used_dates.shape[0], dtype=jnp.int32)
    living = (slot_index % slot_count < jnp.take(used_counts, slot_index // slot_count)).astype(
        jnp.float32
    )
    primary = jnp.take(base, used_dates[:, 0], axis=0)
    secondary = jnp.take(base, used_dates[:, 1], axis=0)
    p_real = primary[:, 0].astype(jnp.float32)
    p_imag = primary[:, 1].astype(jnp.float32)
    s_real = secondary[:, 0].astype(jnp.float32)
    s_imag = secondary[:, 1].astype(jnp.float32)
    real_part = p_real * s_real + p_imag * s_imag
    imaginary = p_imag * s_real - p_real * s_imag
    products = jnp.stack([real_part, imaginary], axis=1) * living[:, None, None, None]
    products = padded(products, (("col", 3),), 4)
    pair_total = products.shape[0]
    padded_width = products.shape[3]
    half_rows = products.shape[2] // 2
    halved = products.reshape(pair_total, 2, half_rows, 2, padded_width).sum(axis=3) * 0.5
    looked = jnp.dot(
        halved.reshape(-1, padded_width),
        look_matrix(padded_width, looks_here),
        precision=lax.Precision.HIGHEST,
        preferred_element_type=jnp.float32,
    )
    looked = looked.reshape(pair_total, 2, half_rows, looks_here)
    return jnp.einsum("qk,kcrm->qcrm", inverse, looked, precision=lax.Precision.HIGHEST)


def per_device(scenes, pair_dates, pair_count, inverse):
    D, C = lax.axis_size("date"), lax.axis_size("col")
    A, _, rows, X = scenes.shape
    S, NP = pair_dates.shape[0], inverse.shape[0]
    R = rows // D
    half = R // 2
    block = A * A * half
    fits = R % 16 == 0 and X % 128 == 0 and X // 8 <= 64 and D & (D - 1) == 0 and 1 < D and S % 8 == 0 and S <= 128
    fits = fits and block % 128 == 0 and A * (A - 1) // 2 * half <= block // 2 and (block // 2) % 16 == 0 and 8 * 2 * A <= 128
    if not fits or D > 8:
        return plain_device(scenes, pair_dates, pair_count, inverse)
    order_in = list(range(1, D))
    cfg = dict(D=D, C=C, A=A, R=R, X=X, S=S, NP=NP, order_in=order_in, send_order=order_in, place_of=place_of(D))
    total = len(chunk_list(order_in)) * block
    TT = X // 128 + 1
    dma = pltpu.SemaphoreType.DMA
    vmem = pl.BlockSpec(memory_space=pltpu.VMEM)
    return pl.pallas_call(
        functools.partial(stack_kernel, cfg),
        out_shape=jax.ShapeDtypeStruct((NP, 2, half, X // 8), F32),
        in_specs=[pl.BlockSpec(memory_space=pl.ANY), vmem, vmem, vmem],
        out_specs=vmem,
        scratch_shapes=[
            pltpu.VMEM(scenes.shape, BF16),
            pltpu.VMEM((D, A, 2, R, X), BF16),
            pltpu.VMEM((D, 2, S), jnp.int32),
            pltpu.VMEM((D, 1, 1), jnp.int32),
            pltpu.VMEM((2, rows, 128), BF16),
            pltpu.VMEM((2, D, R, 128), BF16),
            pltpu.VMEM((2 * TT * A * R, 128), F32),
            pltpu.VMEM((2, 2 * TT, D * A, half, 128), F32),
            pltpu.VMEM((total, 2 * TT * 128), BF16),
            pltpu.VMEM((total, 2 * TT * 128), BF16),
            pltpu.VMEM((2 * TT * 128, 128), BF16),
            pltpu.VMEM((NP * half, total), BF16),
            pltpu.VMEM((NP * half, total), BF16),
            pltpu.VMEM((total, 128), BF16),
            pltpu.VMEM((total, 128), BF16),
            dma, dma((D,)), dma((D,)), dma((D,)), dma((D,)), dma((D,)), dma((D,)), dma((2, D)), dma((2, D)),
        ],
        compiler_params=pltpu.CompilerParams(collective_id=0, has_side_effects=True),
    )(scenes, pair_dates.T, pair_count.reshape(1, 1), inverse)


def place_of(D):
    def combine(place, slot):
        out, bit = 0, 1
        while bit < D:
            a, b = (place // bit) % 2, (slot // bit) % 2
            out = out + bit * (a + b - 2 * a * b)
            bit *= 2
        return out
    return combine


def solution(mesh):
    placed = (P("date", None, "groups", "col"), P("date", None), P("date"), P())
    return jax.shard_map(
        per_device,
        mesh=mesh,
        in_specs=placed,
        out_specs=P(None, None, ("groups", "date"), "col"),
        check_vma=False,
    )
```

```python
import functools

import jax
import jax.numpy as jnp
from jax import lax
from jax.experimental import pallas as pl
from jax.experimental.pallas import tpu as pltpu
from jax.sharding import PartitionSpec as P

MESH = pl.DeviceIdType.MESH
F32 = jnp.float32
BF16 = jnp.bfloat16
EDGE = 4


def flipped(place, slot):
    bit = 1
    out = place
    while bit <= slot:
        if slot & bit:
            out = out + bit - 2 * bit * ((place // bit) % 2)
        bit *= 2
    return out


def split(value):
    high = value.astype(BF16)
    return high, (value - high.astype(F32)).astype(BF16)


def iota(shape, dim):
    return lax.broadcasted_iota(jnp.int32, shape, dim)


def stack_kernel(
    cfg,
    scenes, dates, count, inverse, out,
    local, base, dates_in, counts_in, edge_out, edge_in,
    raw, cells, h_high, h_low, weights, k_high, k_low, l_high, l_low,
    load_sem, send_sem, recv_sem, dates_send, dates_recv, count_send, count_recv, edge_send, edge_recv,
    inverse_in, own_sem,
):
    D, C, A, R, X, S, NP = (cfg[k] for k in ("D", "C", "A", "R", "X", "S", "NP"))
    dates_total = D * A
    T = X // 128
    TT = T + 1
    half = R // 2
    looks = X // 8
    block = A * A * half
    diag = block // 2
    date = lax.axis_index("date")
    col = lax.axis_index("col")
    has_left = col > 0
    has_right = col < C - 1

    barrier = pltpu.get_barrier_semaphore()
    for r in range(1, D):
        pl.semaphore_signal(barrier, inc=1, device_id={"date": flipped(date, r)}, device_id_type=MESH)

    @pl.when(has_left)
    def _():
        for r in range(D):
            pl.semaphore_signal(barrier, inc=1, device_id={"date": flipped(date, r), "col": col - 1}, device_id_type=MESH)

    @pl.when(has_right)
    def _():
        for r in range(D):
            pl.semaphore_signal(barrier, inc=1, device_id={"date": flipped(date, r), "col": col + 1}, device_id_type=MESH)

    load = pltpu.make_async_copy(scenes, local, load_sem)
    load.start()
    own = [
        pltpu.make_async_copy(dates, dates_in.at[date], own_sem.at[0]),
        pltpu.make_async_copy(count, counts_in.at[date], own_sem.at[1]),
        pltpu.make_async_copy(inverse, inverse_in, own_sem.at[2]),
    ]

    for copy in own:
        copy.start()

    load.wait()
    lane = iota((D * R, 128), 1)
    to_left = jnp.zeros((D * R, 128), F32)
    to_right = jnp.zeros((D * R, 128), F32)
    for i in range(2 * A):
        first = local[i // 2, i % 2, :, 0:128].astype(F32)
        last = local[i // 2, i % 2, :, X - 128:X].astype(F32)
        shift = (8 * i + EDGE) % 128
        to_left = jnp.where(lane // EDGE == 2 * i + 1, pltpu.roll(first, shift, 1), to_left)
        shift = (8 * i + EDGE) % 128
        to_right = jnp.where(lane // EDGE == 2 * i, pltpu.roll(last, shift, 1), to_right)
    edge_out[0] = to_right.astype(BF16)
    edge_out[1] = to_left.astype(BF16)

    @pl.when(jnp.logical_not(has_left))
    def _():
        edge_in[0] = jnp.zeros((D, R, 128), BF16)

    @pl.when(jnp.logical_not(has_right))
    def _():
        edge_in[1] = jnp.zeros((D, R, 128), BF16)

    pl.semaphore_wait(barrier, D - 1 + D * (has_left.astype(jnp.int32) + has_right.astype(jnp.int32)))

    def rows_of(place):
        return pl.ds(pl.multiple_of(place * R, R), R)

    def remote(src, dst, ssem, rsem, device):
        return pltpu.make_async_remote_copy(src_ref=src, dst_ref=dst, send_sem=ssem, recv_sem=rsem, device_id=device, device_id_type=MESH)

    to_next = {}
    order = list(range(D - 1, 0, -1))
    for r in range(1, D):
        there = flipped(date, r)
        to_next["dates", r] = remote(dates, dates_in.at[date], dates_send.at[r], dates_recv.at[r], {"date": there})
        to_next["count", r] = remote(count, counts_in.at[date], count_send.at[r], count_recv.at[r], {"date": there})
        to_next["scene", r] = remote(scenes.at[:, :, rows_of(there), :], base.at[r], send_sem.at[r], recv_sem.at[r], {"date": there})
    for r in range(D):
        there = flipped(date, r)
        to_next["right", r] = remote(edge_out.at[0, rows_of(there)], edge_in.at[0, r], edge_send.at[0, r], edge_recv.at[0, r], {"date": there, "col": col + 1})
        to_next["left", r] = remote(edge_out.at[1, rows_of(there)], edge_in.at[1, r], edge_send.at[1, r], edge_recv.at[1, r], {"date": there, "col": col - 1})
    for r in order:
        to_next["dates", r].start()
        to_next["count", r].start()

    @pl.when(has_right)
    def _():
        for r in order + [0]:
            to_next["right", r].start()

    @pl.when(has_left)
    def _():
        for r in order + [0]:
            to_next["left", r].start()

    for r in cfg["send_order"]:
        to_next["scene", r].start()

    row = iota((TT * 128, 128), 0)
    spot = row - TT * 128 + 128
    column = jnp.where(spot < 0, row, jnp.where(spot < EDGE, spot - EDGE, spot - EDGE + X))
    usable = (spot < 2 * EDGE)
    target = iota((TT * 128, 128), 1)
    for c in range(2):
        look = target - 64 * c
        offset = column - 8 * look + 4
        inside = usable & (look >= 0) & (look < looks) & (offset >= 0) & (offset < 16)
        value = jnp.where(inside, (8.0 - jnp.abs(offset.astype(F32) - 7.5)) / 128.0, 0.0)
        weights[c * TT * 128:(c + 1) * TT * 128, :] = value.astype(BF16)

    def unpack(slot, main):
        for c in range(2):
            for t in range(T):
                for i in range(A):
                    at = ((c * TT + t) * A + i) * R
                    raw[at:at + R, :] = main(i, c)[:, t * 128:(t + 1) * 128].astype(F32)
        edges = edge_in[0, slot].astype(F32) + edge_in[1, slot].astype(F32)
        for c in range(2):
            for i in range(A):
                at = ((c * TT + T) * A + i) * R
                shift = (128 - 8 * (2 * i + c)) % 128
                raw[at:at + R, :] = pltpu.roll(edges, shift, 1) if shift else edges
        total = 2 * TT * A * half
        for parity in range(2):
            got = raw[pl.ds(parity, total, stride=2), :]
            cells[parity, :, slot * A:(slot + 1) * A] = got.reshape(2 * TT, A, half, 128)

    def emit(at, pieces):
        rows = pieces[0][0].shape[0]
        for t, both in enumerate(pieces):
            for c in range(2):
                high, low = split(both[c])
                h_high[at:at + rows, (c * TT + t) * 128:(c * TT + t + 1) * 128] = high
                h_low[at:at + rows, (c * TT + t) * 128:(c * TT + t + 1) * 128] = low

    def product(p_of, s_of, t):
        real = imaginary = None
        for parity in range(2):
            p0, p1 = p_of(parity, t), p_of(parity, TT + t)
            s0, s1 = s_of(parity, t), s_of(parity, TT + t)
            one = p0 * s0 + p1 * s1
            two = p1 * s0 - p0 * s1
            real = one if real is None else real + one
            imaginary = two if imaginary is None else imaginary + two
        return real, imaginary

    def pair_order(ra, rb):
        bit = 1
        while 2 * bit <= (ra ^ rb):
            bit *= 2
        swap = (flipped(date, ra) // bit) % 2
        low = ra + swap * (rb - ra)
        high = rb - swap * (rb - ra)
        return low, high

    chunks = []

    def cross(ra, rb):
        at = len(chunks) * block
        chunks.append((ra, rb))
        low, high = pair_order(ra, rb)
        for i in range(A):
            pieces = []
            for t in range(TT):
                both = product(
                    lambda q, n: cells[q, n, low * A + i][None],
                    lambda q, n: cells[q, n, pl.ds(high * A, A)], t)
                pieces.append([v.reshape(A * half, 128) for v in both])
            emit(at + i * A * half, pieces)

    def within(ra):
        at = len(chunks) * block
        chunks.append((ra, ra + 1))
        for side in range(2):
            slot = ra + side
            pieces = []
            for t in range(TT):
                parts = [], []
                for step in range(1, A):
                    both = product(
                        lambda q, n: cells[q, n, slot * A:slot * A + A - step],
                        lambda q, n: cells[q, n, slot * A + step:slot * A + A], t)
                    for c in range(2):
                        parts[c].append(both[c].reshape((A - step) * half, 128))
                pad = jnp.zeros((diag - A * (A - 1) // 2 * half, 128), F32)
                pieces.append([jnp.concatenate(parts[c] + [pad], axis=0) for c in range(2)])
            emit(at + side * diag, pieces)

    def look(start, stop):
        rows = slice(start * block, stop * block)
        got = jnp.dot(h_high[rows, :], weights[...], preferred_element_type=F32)
        got = got + jnp.dot(h_low[rows, :], weights[...], preferred_element_type=F32)
        l_high[rows, :], l_low[rows, :] = split(got)

    def wait_edges(r):
        @pl.when(has_left)
        def _():
            to_next["right", r].wait_recv()

        @pl.when(has_right)
        def _():
            to_next["left", r].wait_recv()

    wait_edges(0)
    unpack(0, lambda i, c: local[i, c, rows_of(date), :])

    order_in = cfg["order_in"]
    looked = 0
    arrived = [0]
    for r in order_in:
        if r == order_in[0]:
            for copy in own:
                copy.wait()
            for q in range(1, D):
                to_next["dates", q].wait_recv()
                to_next["count", q].wait_recv()
        wait_edges(r)
        to_next["scene", r].wait_recv()
        unpack(r, lambda i, c: base[r, i, c])
        if (r ^ 1) in arrived:
            within(r & ~1)
        for other in arrived:
            cross(min(other, r), max(other, r))
        arrived.append(r)
        look(looked, len(chunks))
        looked = len(chunks)
        if r == order_in[0]:
            invert_matrix(cfg, date, dates_in, counts_in, inverse_in, k_high, k_low, pair_order)

    lh, ll = l_high[...], l_low[...]
    kh = k_high[...]
    series = jnp.dot(kh, lh, preferred_element_type=F32)
    series = series + jnp.dot(kh, ll, preferred_element_type=F32)
    series = series + jnp.dot(k_low[...], lh, preferred_element_type=F32)
    for c in range(2):
        out[:, c] = series[:, c * 64:c * 64 + looks].reshape(NP, half, looks)

    for r in range(1, D):
        for kind in ("dates", "count", "scene"):
            to_next[kind, r].wait_send()

    @pl.when(has_right)
    def _():
        for r in range(D):
            to_next["right", r].wait_send()

    @pl.when(has_left)
    def _():
        for r in range(D):
            to_next["left", r].wait_send()


def chunk_list(order_in):
    chunks, arrived = [], [0]
    for r in order_in:
        if (r ^ 1) in arrived:
            chunks.append((r & ~1, None))
        for other in arrived:
            chunks.append((min(other, r), max(other, r)))
        arrived.append(r)
    return chunks


def invert_matrix(cfg, date, dates_in, counts_in, inverse, k_high, k_low, pair_order):
    D, A, R, S, NP = (cfg[k] for k in ("D", "A", "R", "S", "NP"))
    half = R // 2
    block = A * A * half
    diag = block // 2
    total = D * A
    codes = []
    for d in range(D):
        row = dates_in[d, 0:1, :] * total + dates_in[d, 1:2, :]
        live = iota((1, S), 1) < counts_in[d]
        codes.append(jnp.where(live, row, -1).astype(F32))
    codes.append(jnp.full((8 - D % 8 if D % 8 else 8, S), -1.0, F32))
    table = jnp.concatenate(codes, axis=0)
    table = jnp.concatenate([table, jnp.full((table.shape[0], 128 - S), -1.0, F32)], axis=1)
    turned = jnp.transpose(table)
    code = jnp.concatenate([turned[0:S, d:d + 1] for d in range(D)], axis=0).astype(jnp.int32)
    inv = inverse[...]
    spread = jnp.broadcast_to(inv[:, None, :], (NP, half, D * S)).reshape(NP * half, D * S)
    spread_high, spread_low = split(spread)
    place = iota((1, block), 1)
    same = (iota((NP * half, block), 0) % half) == (iota((NP * half, block), 1) % half)
    for n, (ra, rb) in enumerate(chunk_list(cfg["order_in"])):
        if rb is None:
            slot = place // diag
            index = (place % diag) // half
            first = jnp.zeros_like(place)
            second = jnp.zeros_like(place) - 1
            at = 0
            for step in range(1, A):
                for i in range(A - step):
                    first = jnp.where(index == at, i, first)
                    second = jnp.where(index == at, i + step, second)
                    at += 1
            owner = jnp.where(slot == 0, flipped(date, ra), flipped(date, ra + 1))
            want = jnp.where(second >= 0, (owner * A + first) * total + owner * A + second, -2)
        else:
            low, high = pair_order(ra, rb)
            lo_date, hi_date = cfg["place_of"](date, low), cfg["place_of"](date, high)
            first = lo_date * A + place // (A * half)
            second = hi_date * A + (place // half) % A
            want = first * total + second
        hit = jnp.where(code == want, 1.0, 0.0).astype(BF16)
        value = jnp.dot(spread_high, hit, preferred_element_type=F32) + jnp.dot(spread_low, hit, preferred_element_type=F32)
        value = jnp.where(same, value, 0.0)
        columns = slice(n * block, (n + 1) * block)
        k_high[:, columns], k_low[:, columns] = split(value)


def padded(cells, sides, width):
    for axis, dim in sides:
        count = lax.axis_size(axis)
        ends = count - 1
        head = lax.slice_in_dim(cells, 0, width, axis=dim)
        tail = lax.slice_in_dim(cells, cells.shape[dim] - width, cells.shape[dim], axis=dim)
        cells = jnp.concatenate(
            [
                lax.ppermute(tail, axis, [(i, (i + 1) % count) for i in range(ends)]),
                cells,
                lax.ppermute(head, axis, [((i + 1) % count, i) for i in range(ends)]),
            ],
            axis=dim,
        )
    return cells


def look_matrix(padded_width, looks_here):
    column = jnp.arange(padded_width, dtype=jnp.int32)[:, None]
    target = jnp.arange(looks_here, dtype=jnp.int32)[None, :]
    offset = (column - 8 * target).astype(jnp.float32)
    inside = (offset >= 0.0) & (offset < 16.0)
    return jnp.where(inside, (8.0 - jnp.abs(offset - 7.5)) / 64.0, 0.0)


def plain_device(scenes, pair_dates, pair_count, inverse):
    slot_count = pair_dates.shape[0]
    looks_here = scenes.shape[3] // 8
    base = lax.all_to_all(scenes, "date", split_axis=2, concat_axis=0, tiled=True)
    used_dates, used_counts = (
        lax.all_gather(pair_dates, "date", axis=0, tiled=True),
        lax.all_gather(pair_count, "date", axis=0, tiled=True),
    )
    slot_index = jnp.arange(used_dates.shape[0], dtype=jnp.int32)
    living = (slot_index % slot_count < jnp.take(used_counts, slot_index // slot_count)).astype(
        jnp.float32
    )
    primary = jnp.take(base, used_dates[:, 0], axis=0)
    secondary = jnp.take(base, used_dates[:, 1], axis=0)
    p_real = primary[:, 0].astype(jnp.float32)
    p_imag = primary[:, 1].astype(jnp.float32)
    s_real = secondary[:, 0].astype(jnp.float32)
    s_imag = secondary[:, 1].astype(jnp.float32)
    real_part = p_real * s_real + p_imag * s_imag
    imaginary = p_imag * s_real - p_real * s_imag
    products = jnp.stack([real_part, imaginary], axis=1) * living[:, None, None, None]
    products = padded(products, (("col", 3),), 4)
    pair_total = products.shape[0]
    padded_width = products.shape[3]
    half_rows = products.shape[2] // 2
    halved = products.reshape(pair_total, 2, half_rows, 2, padded_width).sum(axis=3) * 0.5
    looked = jnp.dot(
        halved.reshape(-1, padded_width),
        look_matrix(padded_width, looks_here),
        precision=lax.Precision.HIGHEST,
        preferred_element_type=jnp.float32,
    )
    looked = looked.reshape(pair_total, 2, half_rows, looks_here)
    return jnp.einsum("qk,kcrm->qcrm", inverse, looked, precision=lax.Precision.HIGHEST)


def per_device(scenes, pair_dates, pair_count, inverse):
    D, C = lax.axis_size("date"), lax.axis_size("col")
    A, _, rows, X = scenes.shape
    S, NP = pair_dates.shape[0], inverse.shape[0]
    R = rows // D
    half = R // 2
    block = A * A * half
    fits = R % 16 == 0 and X % 128 == 0 and X // 8 <= 64 and D & (D - 1) == 0 and 1 < D and S % 8 == 0 and S <= 128
    fits = fits and block % 128 == 0 and A * (A - 1) // 2 * half <= block // 2 and (block // 2) % 16 == 0 and 8 * 2 * A <= 128
    if not fits or D > 8:
        return plain_device(scenes, pair_dates, pair_count, inverse)
    order_in = list(range(1, D))
    cfg = dict(D=D, C=C, A=A, R=R, X=X, S=S, NP=NP, order_in=order_in, send_order=order_in, place_of=place_of(D))
    total = len(chunk_list(order_in)) * block
    TT = X // 128 + 1
    dma = pltpu.SemaphoreType.DMA
    vmem = pl.BlockSpec(memory_space=pltpu.VMEM)
    return pl.pallas_call(
        functools.partial(stack_kernel, cfg),
        out_shape=pltpu.VMEM((NP, 2, half, X // 8), F32),
        in_specs=[pl.BlockSpec(memory_space=pltpu.HBM)] * 4,
        out_specs=vmem,
        scratch_shapes=[
            pltpu.VMEM(scenes.shape, BF16),
            pltpu.VMEM((D, A, 2, R, X), BF16),
            pltpu.VMEM((D, 2, S), jnp.int32),
            pltpu.VMEM((D, 1, 1), jnp.int32),
            pltpu.VMEM((2, rows, 128), BF16),
            pltpu.VMEM((2, D, R, 128), BF16),
            pltpu.VMEM((2 * TT * A * R, 128), F32),
            pltpu.VMEM((2, 2 * TT, D * A, half, 128), F32),
            pltpu.VMEM((total, 2 * TT * 128), BF16),
            pltpu.VMEM((total, 2 * TT * 128), BF16),
            pltpu.VMEM((2 * TT * 128, 128), BF16),
            pltpu.VMEM((NP * half, total), BF16),
            pltpu.VMEM((NP * half, total), BF16),
            pltpu.VMEM((total, 128), BF16),
            pltpu.VMEM((total, 128), BF16),
            dma, dma((D,)), dma((D,)), dma((D,)), dma((D,)), dma((D,)), dma((D,)), dma((2, D)), dma((2, D)),
            pltpu.VMEM(inverse.shape, F32), dma((3,)),
        ],
        compiler_params=pltpu.CompilerParams(collective_id=0, has_side_effects=True),
    )(scenes, pair_dates.T, pair_count.reshape(1, 1), inverse)


def place_of(D):
    def combine(place, slot):
        out, bit = 0, 1
        while bit < D:
            a, b = (place // bit) % 2, (slot // bit) % 2
            out = out + bit * (a + b - 2 * a * b)
            bit *= 2
        return out
    return combine


def solution(mesh):
    placed = (P("date", None, "groups", "col"), P("date", None), P("date"), P())
    return jax.shard_map(
        per_device,
        mesh=mesh,
        in_specs=placed,
        out_specs=P(None, None, ("groups", "date"), "col"),
        check_vma=False,
    )
```

```python
import functools

import jax
import jax.numpy as jnp
from jax import lax
from jax.experimental import pallas as pl
from jax.experimental.pallas import tpu as pltpu
from jax.sharding import PartitionSpec as P

MESH = pl.DeviceIdType.MESH
F32 = jnp.float32
BF16 = jnp.bfloat16
EDGE = 4


def flipped(place, slot):
    bit = 1
    out = place
    while bit <= slot:
        if slot & bit:
            out = out + bit - 2 * bit * ((place // bit) % 2)
        bit *= 2
    return out


def split(value):
    high = value.astype(BF16)
    return high, (value - high.astype(F32)).astype(BF16)


def iota(shape, dim):
    return lax.broadcasted_iota(jnp.int32, shape, dim)


def stack_kernel(
    cfg,
    scenes, dates, count, inverse, out,
    local, base, dates_in, counts_in, edge_out, edge_in,
    raw, cells, total, h_high, h_low, weights, k_high, k_low, l_high, l_low,
    load_sem, send_sem, recv_sem, dates_send, dates_recv, count_send, count_recv, edge_send, edge_recv,
    inverse_in, own_sem, edge_near, near_send, near_recv,
):
    D, C, A, R, X, S, NP = (cfg[k] for k in ("D", "C", "A", "R", "X", "S", "NP"))
    T = X // 128
    TT = T + 1
    half = R // 2
    looks = X // 8
    date = lax.axis_index("date")
    col = lax.axis_index("col")
    has_left = col > 0
    has_right = col < C - 1

    barrier = pltpu.get_barrier_semaphore()
    for r in range(1, D):
        pl.semaphore_signal(barrier, inc=1, device_id={"date": flipped(date, r)}, device_id_type=MESH)

    @pl.when(has_left)
    def _():
        pl.semaphore_signal(barrier, inc=1, device_id={"col": col - 1}, device_id_type=MESH)

    @pl.when(has_right)
    def _():
        pl.semaphore_signal(barrier, inc=1, device_id={"col": col + 1}, device_id_type=MESH)

    load = pltpu.make_async_copy(scenes, local, load_sem)
    load.start()
    own = [
        pltpu.make_async_copy(dates, dates_in.at[date], own_sem.at[0]),
        pltpu.make_async_copy(count, counts_in.at[date], own_sem.at[1]),
        pltpu.make_async_copy(inverse, inverse_in, own_sem.at[2]),
    ]

    for copy in own:
        copy.start()

    load.wait()
    lane = iota((D * R, 128), 1)
    to_left = jnp.zeros((D * R, 128), F32)
    to_right = jnp.zeros((D * R, 128), F32)
    for i in range(2 * A):
        first = local[i // 2, i % 2, :, 0:128].astype(F32)
        last = local[i // 2, i % 2, :, X - 128:X].astype(F32)
        shift = (8 * i + EDGE) % 128
        to_left = jnp.where(lane // EDGE == 2 * i + 1, pltpu.roll(first, shift, 1), to_left)
        shift = (8 * i + EDGE) % 128
        to_right = jnp.where(lane // EDGE == 2 * i, pltpu.roll(last, shift, 1), to_right)
    edge_out[0] = to_right.astype(BF16)
    edge_out[1] = to_left.astype(BF16)

    for side, present in ((0, has_left), (1, has_right)):
        @pl.when(jnp.logical_not(present))
        def _():
            edge_in[side] = jnp.zeros((D, R, 128), BF16)
            edge_near[side] = jnp.zeros((D * R, 128), BF16)

    pl.semaphore_wait(barrier, D - 1 + (has_left.astype(jnp.int32) + has_right.astype(jnp.int32)))

    def rows_of(place):
        return pl.ds(pl.multiple_of(place * R, R), R)

    def remote(src, dst, ssem, rsem, device):
        return pltpu.make_async_remote_copy(src_ref=src, dst_ref=dst, send_sem=ssem, recv_sem=rsem, device_id=device, device_id_type=MESH)

    to_next = {}
    order = list(range(D - 1, 0, -1))
    for r in range(1, D):
        there = flipped(date, r)
        to_next["dates", r] = remote(dates, dates_in.at[date], dates_send.at[r], dates_recv.at[r], {"date": there})
        to_next["count", r] = remote(count, counts_in.at[date], count_send.at[r], count_recv.at[r], {"date": there})
        for begin, end in cfg["cuts"][r]:
            to_next["scene", r, begin] = remote(
                scenes.at[begin:end, :, rows_of(there), :], base.at[r, begin:end],
                send_sem.at[r, begin], recv_sem.at[r, begin], {"date": there})
    near = (
        remote(edge_out.at[0], edge_near.at[0], near_send.at[0], near_recv.at[0], {"col": col + 1}),
        remote(edge_out.at[1], edge_near.at[1], near_send.at[1], near_recv.at[1], {"col": col - 1}),
    )
    for r in range(1, D):
        there = flipped(date, r)
        for side in range(2):
            to_next["edge", side, r] = remote(edge_near.at[side, rows_of(there)], edge_in.at[side, r], edge_send.at[side, r], edge_recv.at[side, r], {"date": there})

    @pl.when(has_right)
    def _():
        near[0].start()

    @pl.when(has_left)
    def _():
        near[1].start()

    order_in = cfg["order_in"]
    early = [r for r in order_in if r <= D // 2]
    late = [r for r in order_in if r > D // 2]
    for r in order_in[::-1]:
        to_next["dates", r].start()
        to_next["count", r].start()
    for r in early:
        for begin, _ in cfg["cuts"][r]:
            to_next["scene", r, begin].start()

    row = iota((TT * 128, 128), 0)
    spot = row - TT * 128 + 128
    column = jnp.where(spot < 0, row, jnp.where(spot < EDGE, spot - EDGE, spot - EDGE + X))
    usable = (spot < 2 * EDGE)
    target = iota((TT * 128, 128), 1)
    for c in range(2):
        look = target - 64 * c
        offset = column - 8 * look + 4
        inside = usable & (look >= 0) & (look < looks) & (offset >= 0) & (offset < 16)
        value = jnp.where(inside, (8.0 - jnp.abs(offset.astype(F32) - 7.5)) / 128.0, 0.0)
        weights[c * TT * 128:(c + 1) * TT * 128, :] = value.astype(BF16)

    for side, present in ((0, has_left), (1, has_right)):
        @pl.when(present)
        def _():
            near[side].wait_recv()
            for r in order_in[::-1]:
                to_next["edge", side, r].start()

    for r in late:
        for begin, _ in cfg["cuts"][r]:
            to_next["scene", r, begin].start()

    def unpack(slot, begin, end, main):
        many = end - begin
        for c in range(2):
            for t in range(T):
                for i in range(many):
                    at = ((c * TT + t) * many + i) * R
                    raw[at:at + R, :] = main(begin + i, c)[:, t * 128:(t + 1) * 128].astype(F32)
        at_edge = [edge_in[n, slot] if slot else edge_near[n, rows_of(date), :] for n in range(2)]
        edges = at_edge[0].astype(F32) + at_edge[1].astype(F32)
        for c in range(2):
            for i in range(many):
                at = ((c * TT + T) * many + i) * R
                shift = (128 - 8 * (2 * (begin + i) + c)) % 128
                raw[at:at + R, :] = pltpu.roll(edges, shift, 1) if shift else edges
        size = 2 * TT * many * half
        for parity in range(2):
            got = raw[pl.ds(parity, size, stride=2), :]
            cells[parity, :, slot * A + begin:slot * A + end] = got.reshape(2 * TT, many, half, 128)

    def wait_edges(r):
        for side, present in ((0, has_left), (1, has_right)):
            @pl.when(present)
            def _():
                to_next["edge", side, r].wait_recv()

    def product(p_at, s_at, t):
        real = imaginary = None
        for parity in range(2):
            p0, p1 = cells[parity, t, p_at][None], cells[parity, TT + t, p_at][None]
            s0, s1 = cells[parity, t, s_at], cells[parity, TT + t, s_at]
            one = p0 * s0 + p1 * s1
            two = p1 * s0 - p0 * s1
            real = one if real is None else real + one
            imaginary = two if imaginary is None else imaginary + two
        return real, imaginary

    lanes = iota((1, 128), 1)

    def multiply(stage):
        at = stage["at"]
        rows = stage["rows"]
        for t in range(TT):
            for c in range(2):
                where = (c * TT + t) * 128
                parts = []
                for r, j, q, n, _ in stage["pieces"]:
                    if c == 0:
                        made[r, j, q, t] = product(r * A + j, slice(q * A, q * A + n), t)
                    parts.append(made[r, j, q, t][c].reshape(n * half, 128))
                if rows > stage["used"]:
                    parts.append(jnp.zeros((rows - stage["used"], 128), F32))
                high, low = split(jnp.concatenate(parts, axis=0))
                h_high[at:at + rows, where:where + 128] = high
                h_low[at:at + rows, where:where + 128] = low
        got = jnp.dot(h_high[at:at + rows, :], weights[...], preferred_element_type=F32)
        got = got + jnp.dot(h_low[at:at + rows, :], weights[...], preferred_element_type=F32)
        signed = []
        for r, j, q, n, start in stage["pieces"]:
            sign = (2 * swapped(date, q, r) - 1).astype(F32) if q != r else -1.0
            signed.append(got[start:start + n * half] * jnp.where(lanes < 64, 1.0, sign))
        if rows > stage["used"]:
            signed.append(got[stage["used"]:rows])
        l_high[at:at + rows, :], l_low[at:at + rows, :] = split(jnp.concatenate(signed, axis=0))

    made = {}

    def invert(start, stop):
        rows = slice(start, stop)
        lh, ll = l_high[rows, :], l_low[rows, :]
        kh = k_high[:, rows]
        part = jnp.dot(kh, lh, preferred_element_type=F32)
        part = part + jnp.dot(kh, ll, preferred_element_type=F32)
        return part + jnp.dot(k_low[:, rows], lh, preferred_element_type=F32)

    stages = cfg["stages"]
    for stage in stages:
        if stage["padded"] > stage["rows"]:
            gap = slice(stage["at"] + stage["rows"], stage["at"] + stage["padded"])
            l_high[gap, :] = jnp.zeros((stage["padded"] - stage["rows"], 128), BF16)
            l_low[gap, :] = jnp.zeros((stage["padded"] - stage["rows"], 128), BF16)

    unpack(0, 0, A, lambda i, c: local[i, c, rows_of(date), :])
    for copy in own:
        copy.wait()
    for q in range(1, D):
        to_next["dates", q].wait_recv()
        to_next["count", q].wait_recv()
    invert_matrix(cfg, date, dates_in, counts_in, inverse_in, k_high, k_low)

    for n, stage in enumerate(stages):
        for r, begin, end in stage["arrive"]:
            if begin == 0:
                wait_edges(r)
            to_next["scene", r, begin].wait_recv()
            unpack(r, begin, end, lambda i, c: base[r, i, c])
        multiply(stage)
        if n == len(stages) - 2:
            total[...] = invert(0, stage["at"] + stage["padded"])
    series = invert(stages[-1]["at"], stages[-1]["at"] + stages[-1]["padded"])
    if len(stages) > 1:
        series = series + total[...]
    for c in range(2):
        out[:, c] = series[:, c * 64:c * 64 + looks].reshape(NP, half, looks)

    for key, copy in to_next.items():
        if key[0] in ("dates", "count", "scene"):
            copy.wait_send()

    for side, come, go in ((0, has_left, has_right), (1, has_right, has_left)):
        @pl.when(go)
        def _():
            near[side].wait_send()

        @pl.when(come)
        def _():
            for r in range(1, D):
                to_next["edge", side, r].wait_send()


def swapped(date, low, high):
    bit = 1
    while 2 * bit <= (low ^ high):
        bit *= 2
    return (flipped(date, low) // bit) % 2


def plan(D, A, half):
    cuts = {r: [(0, A)] for r in range(1, D)}
    cuts[D - 1] = [(0, A // 2), (A // 2, A)] if A > 1 else [(0, A)]
    stages, at = [], 0
    for r in range(1, D):
        for begin, end in cuts[r]:
            news = [(r, j) for j in range(begin, end)]
            if r == 1 and begin == 0:
                news = [(0, j) for j in range(A)] + news
            pieces, used = [], 0
            for slot, j in news:
                for q in range(slot + 1):
                    n = A if q < slot else j
                    if n:
                        pieces.append((slot, j, q, n, used))
                        used += n * half
            rows = -(-used // 16) * 16
            padded = -(-used // 128) * 128
            stages.append(dict(arrive=[(r, begin, end)], pieces=pieces, used=used, rows=rows, padded=padded, at=at))
            at += padded
    return cuts, stages, at


def invert_matrix(cfg, date, dates_in, counts_in, inverse, k_high, k_low):
    D, A, R, S, NP = (cfg[k] for k in ("D", "A", "R", "S", "NP"))
    half = R // 2
    total = D * A
    codes = []
    for d in range(D):
        row = dates_in[d, 0:1, :] * total + dates_in[d, 1:2, :]
        live = iota((1, S), 1) < counts_in[d]
        codes.append(jnp.where(live, row, -1).astype(F32))
    codes.append(jnp.full((8 - D % 8 if D % 8 else 8, S), -1.0, F32))
    table = jnp.concatenate(codes, axis=0)
    table = jnp.concatenate([table, jnp.full((table.shape[0], 128 - S), -1.0, F32)], axis=1)
    turned = jnp.transpose(table)
    code = jnp.concatenate([turned[0:S, d:d + 1] for d in range(D)], axis=0).astype(jnp.int32)
    inv = inverse[...]
    spread = jnp.broadcast_to(inv[:, None, :], (NP, half, D * S)).reshape(NP * half, D * S)
    spread_high, spread_low = split(spread)
    for stage in cfg["stages"]:
        width = stage["padded"]
        place = iota((1, width), 1)
        same = (iota((NP * half, width), 0) % half) == (iota((NP * half, width), 1) % half)
        want = jnp.full((1, width), -2, jnp.int32)
        for r, j, q, n, start in stage["pieces"]:
            new, old = flipped(date, r) * A + j, flipped(date, q) * A
            swap = swapped(date, q, r) if q != r else 0
            first = swap * (new * total + old) + (1 - swap) * (old * total + new)
            step = swap + (1 - swap) * total
            inside = (place >= start) & (place < start + n * half)
            want = jnp.where(inside, first + step * ((place - start) // half), want)
        hit = jnp.where(code == want, 1.0, 0.0).astype(BF16)
        value = jnp.dot(spread_high, hit, preferred_element_type=F32) + jnp.dot(spread_low, hit, preferred_element_type=F32)
        value = jnp.where(same, value, 0.0)
        columns = slice(stage["at"], stage["at"] + width)
        k_high[:, columns], k_low[:, columns] = split(value)


def padded(cells, sides, width):
    for axis, dim in sides:
        count = lax.axis_size(axis)
        ends = count - 1
        head = lax.slice_in_dim(cells, 0, width, axis=dim)
        tail = lax.slice_in_dim(cells, cells.shape[dim] - width, cells.shape[dim], axis=dim)
        cells = jnp.concatenate(
            [
                lax.ppermute(tail, axis, [(i, (i + 1) % count) for i in range(ends)]),
                cells,
                lax.ppermute(head, axis, [((i + 1) % count, i) for i in range(ends)]),
            ],
            axis=dim,
        )
    return cells


def look_matrix(padded_width, looks_here):
    column = jnp.arange(padded_width, dtype=jnp.int32)[:, None]
    target = jnp.arange(looks_here, dtype=jnp.int32)[None, :]
    offset = (column - 8 * target).astype(jnp.float32)
    inside = (offset >= 0.0) & (offset < 16.0)
    return jnp.where(inside, (8.0 - jnp.abs(offset - 7.5)) / 64.0, 0.0)


def plain_device(scenes, pair_dates, pair_count, inverse):
    slot_count = pair_dates.shape[0]
    looks_here = scenes.shape[3] // 8
    base = lax.all_to_all(scenes, "date", split_axis=2, concat_axis=0, tiled=True)
    used_dates, used_counts = (
        lax.all_gather(pair_dates, "date", axis=0, tiled=True),
        lax.all_gather(pair_count, "date", axis=0, tiled=True),
    )
    slot_index = jnp.arange(used_dates.shape[0], dtype=jnp.int32)
    living = (slot_index % slot_count < jnp.take(used_counts, slot_index // slot_count)).astype(
        jnp.float32
    )
    primary = jnp.take(base, used_dates[:, 0], axis=0)
    secondary = jnp.take(base, used_dates[:, 1], axis=0)
    p_real = primary[:, 0].astype(jnp.float32)
    p_imag = primary[:, 1].astype(jnp.float32)
    s_real = secondary[:, 0].astype(jnp.float32)
    s_imag = secondary[:, 1].astype(jnp.float32)
    real_part = p_real * s_real + p_imag * s_imag
    imaginary = p_imag * s_real - p_real * s_imag
    products = jnp.stack([real_part, imaginary], axis=1) * living[:, None, None, None]
    products = padded(products, (("col", 3),), 4)
    pair_total = products.shape[0]
    padded_width = products.shape[3]
    half_rows = products.shape[2] // 2
    halved = products.reshape(pair_total, 2, half_rows, 2, padded_width).sum(axis=3) * 0.5
    looked = jnp.dot(
        halved.reshape(-1, padded_width),
        look_matrix(padded_width, looks_here),
        precision=lax.Precision.HIGHEST,
        preferred_element_type=jnp.float32,
    )
    looked = looked.reshape(pair_total, 2, half_rows, looks_here)
    return jnp.einsum("qk,kcrm->qcrm", inverse, looked, precision=lax.Precision.HIGHEST)


def per_device(scenes, pair_dates, pair_count, inverse):
    D, C = lax.axis_size("date"), lax.axis_size("col")
    A, _, rows, X = scenes.shape
    S, NP = pair_dates.shape[0], inverse.shape[0]
    R = rows // D
    half = R // 2
    fits = R % 16 == 0 and X % 128 == 0 and X // 8 <= 64 and D & (D - 1) == 0 and 1 < D <= 8
    fits = fits and S % 8 == 0 and S <= 128 and 16 * A <= 128
    if not fits:
        return plain_device(scenes, pair_dates, pair_count, inverse)
    cuts, stages, total = plan(D, A, half)
    cfg = dict(D=D, C=C, A=A, R=R, X=X, S=S, NP=NP, order_in=list(range(1, D)), cuts=cuts, stages=stages)
    TT = X // 128 + 1
    dma = pltpu.SemaphoreType.DMA
    vmem = pl.BlockSpec(memory_space=pltpu.VMEM)
    return pl.pallas_call(
        functools.partial(stack_kernel, cfg),
        out_shape=pltpu.VMEM((NP, 2, half, X // 8), F32),
        in_specs=[pl.BlockSpec(memory_space=pltpu.HBM)] * 4,
        out_specs=vmem,
        scratch_shapes=[
            pltpu.VMEM(scenes.shape, BF16),
            pltpu.VMEM((D, A, 2, R, X), BF16),
            pltpu.VMEM((D, 2, S), jnp.int32),
            pltpu.VMEM((D, 1, 1), jnp.int32),
            pltpu.VMEM((2, rows, 128), BF16),
            pltpu.VMEM((2, D, R, 128), BF16),
            pltpu.VMEM((2 * TT * A * R, 128), F32),
            pltpu.VMEM((2, 2 * TT, D * A, half, 128), F32),
            pltpu.VMEM((NP * half, 128), F32),
            pltpu.VMEM((total, 2 * TT * 128), BF16),
            pltpu.VMEM((total, 2 * TT * 128), BF16),
            pltpu.VMEM((2 * TT * 128, 128), BF16),
            pltpu.VMEM((NP * half, total), BF16),
            pltpu.VMEM((NP * half, total), BF16),
            pltpu.VMEM((total, 128), BF16),
            pltpu.VMEM((total, 128), BF16),
            dma, dma((D, A)), dma((D, A)), dma((D,)), dma((D,)), dma((D,)), dma((D,)), dma((2, D)), dma((2, D)),
            pltpu.VMEM(inverse.shape, F32), dma((3,)), pltpu.VMEM((2, rows, 128), BF16), dma((2,)), dma((2,)),
        ],
        compiler_params=pltpu.CompilerParams(collective_id=0, has_side_effects=True),
    )(scenes, pair_dates.T, pair_count.reshape(1, 1), inverse)


def solution(mesh):
    placed = (P("date", None, "groups", "col"), P("date", None), P("date"), P())
    return jax.shard_map(
        per_device,
        mesh=mesh,
        in_specs=placed,
        out_specs=P(None, None, ("groups", "date"), "col"),
        check_vma=False,
    )
```

```python
import functools

import jax
import jax.numpy as jnp
from jax import lax
from jax.experimental import pallas as pl
from jax.experimental.pallas import tpu as pltpu
from jax.sharding import PartitionSpec as P

MESH = pl.DeviceIdType.MESH
F32 = jnp.float32
BF16 = jnp.bfloat16
EDGE = 4


def flipped(place, slot):
    bit = 1
    out = place
    while bit <= slot:
        if slot & bit:
            out = out + bit - 2 * bit * ((place // bit) % 2)
        bit *= 2
    return out


def split(value):
    high = value.astype(BF16)
    return high, (value - high.astype(F32)).astype(BF16)


def iota(shape, dim):
    return lax.broadcasted_iota(jnp.int32, shape, dim)


def stack_kernel(
    cfg,
    scenes, dates, count, inverse, out,
    local, base, dates_in, counts_in, edge_out, edge_in,
    raw, cells, total, h_high, h_low, weights, k_high, k_low, l_high, l_low,
    load_sem, send_sem, recv_sem, dates_send, dates_recv, count_send, count_recv, edge_send, edge_recv,
    inverse_in, own_sem, looked,
):
    D, C, A, R, X, S, NP = (cfg[k] for k in ("D", "C", "A", "R", "X", "S", "NP"))
    T = X // 128
    TT = T + 1
    half = R // 2
    looks = X // 8
    date = lax.axis_index("date")
    col = lax.axis_index("col")
    has_left = col > 0
    has_right = col < C - 1

    barrier = pltpu.get_barrier_semaphore()
    for r in range(1, D):
        pl.semaphore_signal(barrier, inc=1, device_id={"date": flipped(date, r)}, device_id_type=MESH)

    @pl.when(has_left)
    def _():
        for r in range(D):
            pl.semaphore_signal(barrier, inc=1, device_id={"date": flipped(date, r), "col": col - 1}, device_id_type=MESH)

    @pl.when(has_right)
    def _():
        for r in range(D):
            pl.semaphore_signal(barrier, inc=1, device_id={"date": flipped(date, r), "col": col + 1}, device_id_type=MESH)

    load = pltpu.make_async_copy(scenes, local, load_sem)
    load.start()
    own = [
        pltpu.make_async_copy(dates, dates_in.at[date], own_sem.at[0]),
        pltpu.make_async_copy(count, counts_in.at[date], own_sem.at[1]),
        pltpu.make_async_copy(inverse, inverse_in, own_sem.at[2]),
    ]

    for copy in own:
        copy.start()

    load.wait()
    lane = iota((D * R, 128), 1)
    to_left = jnp.zeros((D * R, 128), F32)
    to_right = jnp.zeros((D * R, 128), F32)
    for i in range(2 * A):
        first = local[i // 2, i % 2, :, 0:128].astype(F32)
        last = local[i // 2, i % 2, :, X - 128:X].astype(F32)
        shift = (8 * i + EDGE) % 128
        to_left = jnp.where(lane // EDGE == 2 * i + 1, pltpu.roll(first, shift, 1), to_left)
        shift = (8 * i + EDGE) % 128
        to_right = jnp.where(lane // EDGE == 2 * i, pltpu.roll(last, shift, 1), to_right)
    edge_out[0] = to_right.astype(BF16)
    edge_out[1] = to_left.astype(BF16)

    @pl.when(jnp.logical_not(has_left))
    def _():
        edge_in[0] = jnp.zeros((D, R, 128), BF16)

    @pl.when(jnp.logical_not(has_right))
    def _():
        edge_in[1] = jnp.zeros((D, R, 128), BF16)

    pl.semaphore_wait(barrier, D - 1 + D * (has_left.astype(jnp.int32) + has_right.astype(jnp.int32)))

    def rows_of(place):
        return pl.ds(pl.multiple_of(place * R, R), R)

    def remote(src, dst, ssem, rsem, device):
        return pltpu.make_async_remote_copy(src_ref=src, dst_ref=dst, send_sem=ssem, recv_sem=rsem, device_id=device, device_id_type=MESH)

    to_next = {}
    order = list(range(D - 1, 0, -1))
    for r in range(1, D):
        there = flipped(date, r)
        to_next["dates", r] = remote(dates, dates_in.at[date], dates_send.at[r], dates_recv.at[r], {"date": there})
        to_next["count", r] = remote(count, counts_in.at[date], count_send.at[r], count_recv.at[r], {"date": there})
        for begin, end in cfg["cuts"][r]:
            to_next["scene", r, begin] = remote(
                scenes.at[begin:end, :, rows_of(there), :], base.at[r, begin:end],
                send_sem.at[r, begin], recv_sem.at[r, begin], {"date": there})
    for r in range(D):
        there = flipped(date, r)
        to_next["right", r] = remote(edge_out.at[0, rows_of(there)], edge_in.at[0, r], edge_send.at[0, r], edge_recv.at[0, r], {"date": there, "col": col + 1})
        to_next["left", r] = remote(edge_out.at[1, rows_of(there)], edge_in.at[1, r], edge_send.at[1, r], edge_recv.at[1, r], {"date": there, "col": col - 1})
    for r in order:
        to_next["dates", r].start()
        to_next["count", r].start()

    @pl.when(has_right)
    def _():
        for r in order + [0]:
            to_next["right", r].start()

    @pl.when(has_left)
    def _():
        for r in order + [0]:
            to_next["left", r].start()

    for r in cfg["order_in"]:
        for begin, _ in cfg["cuts"][r]:
            to_next["scene", r, begin].start()

    row = iota((TT * 128, 128), 0)
    spot = row - TT * 128 + 128
    column = jnp.where(spot < 0, row, jnp.where(spot < EDGE, spot - EDGE, spot - EDGE + X))
    usable = (spot < 2 * EDGE)
    target = iota((TT * 128, 128), 1)
    for c in range(2):
        look = target - 64 * c
        offset = column - 8 * look + 4
        inside = usable & (look >= 0) & (look < looks) & (offset >= 0) & (offset < 16)
        value = jnp.where(inside, (8.0 - jnp.abs(offset.astype(F32) - 7.5)) / 128.0, 0.0)
        weights[c * TT * 128:(c + 1) * TT * 128, :] = value.astype(BF16)

    def unpack(slot, begin, end, main):
        many = end - begin
        for c in range(2):
            for t in range(T):
                for i in range(many):
                    at = ((c * TT + t) * many + i) * R
                    raw[at:at + R, :] = main(begin + i, c)[:, t * 128:(t + 1) * 128].astype(F32)
        edges = edge_in[0, slot].astype(F32) + edge_in[1, slot].astype(F32)
        for c in range(2):
            for i in range(many):
                at = ((c * TT + T) * many + i) * R
                shift = (128 - 8 * (2 * (begin + i) + c)) % 128
                raw[at:at + R, :] = pltpu.roll(edges, shift, 1) if shift else edges
        size = 2 * TT * many * half
        for parity in range(2):
            got = raw[pl.ds(parity, size, stride=2), :]
            cells[parity, :, slot * A + begin:slot * A + end] = got.reshape(2 * TT, many, half, 128)

    def wait_edges(r):
        @pl.when(has_left)
        def _():
            to_next["right", r].wait_recv()

        @pl.when(has_right)
        def _():
            to_next["left", r].wait_recv()

    def product(p_at, s_at, t):
        real = imaginary = None
        for parity in range(2):
            p0, p1 = cells[parity, t, p_at][None], cells[parity, TT + t, p_at][None]
            s0, s1 = cells[parity, t, s_at], cells[parity, TT + t, s_at]
            one = p0 * s0 + p1 * s1
            two = p1 * s0 - p0 * s1
            real = one if real is None else real + one
            imaginary = two if imaginary is None else imaginary + two
        return real, imaginary

    lanes = iota((1, 128), 1)

    def multiply(stage):
        at = stage["at"]
        rows = stage["rows"]
        whole = [[p] for p in stage["pieces"] if p[2] != p[0]]
        rest = [p for p in stage["pieces"] if p[2] == p[0]]
        for group in whole + ([rest] if rest else []):
            begin = at + group[0][4]
            for t in range(TT):
                parts = [product(r * A + j, slice(q * A, q * A + n), t) for r, j, q, n, _ in group]
                for c in range(2):
                    flat = [v[c].reshape(p[3] * half, 128) for v, p in zip(parts, group)]
                    end = begin + sum(p[3] for p in group) * half
                    if group is rest and end < at + rows:
                        flat.append(jnp.zeros((at + rows - end, 128), F32))
                        end = at + rows
                    where = (c * TT + t) * 128
                    high, low = split(flat[0] if len(flat) == 1 else jnp.concatenate(flat, axis=0))
                    h_high[begin:end, where:where + 128] = high
                    h_low[begin:end, where:where + 128] = low
        got = jnp.dot(h_high[at:at + rows, :], weights[...], preferred_element_type=F32)
        got = got + jnp.dot(h_low[at:at + rows, :], weights[...], preferred_element_type=F32)
        for r, j, q, n, start in stage["pieces"]:
            sign = (2 * swapped(date, q, r) - 1).astype(F32) if q != r else -1.0
            looked[start:start + n * half, :] = got[start:start + n * half] * jnp.where(lanes < 64, 1.0, sign)
        if rows > stage["used"]:
            looked[stage["used"]:rows, :] = got[stage["used"]:rows]
        l_high[at:at + rows, :], l_low[at:at + rows, :] = split(looked[0:rows, :])

    def invert(start, stop):
        rows = slice(start, stop)
        lh, ll = l_high[rows, :], l_low[rows, :]
        kh = k_high[:, rows]
        part = jnp.dot(kh, lh, preferred_element_type=F32)
        part = part + jnp.dot(kh, ll, preferred_element_type=F32)
        return part + jnp.dot(k_low[:, rows], lh, preferred_element_type=F32)

    stages = cfg["stages"]
    for stage in stages:
        if stage["padded"] > stage["rows"]:
            gap = slice(stage["at"] + stage["rows"], stage["at"] + stage["padded"])
            l_high[gap, :] = jnp.zeros((stage["padded"] - stage["rows"], 128), BF16)
            l_low[gap, :] = jnp.zeros((stage["padded"] - stage["rows"], 128), BF16)

    wait_edges(0)
    unpack(0, 0, A, lambda i, c: local[i, c, rows_of(date), :])
    for copy in own:
        copy.wait()
    for q in range(1, D):
        to_next["dates", q].wait_recv()
        to_next["count", q].wait_recv()
    invert_matrix(cfg, date, dates_in, counts_in, inverse_in, k_high, k_low)

    for n, stage in enumerate(stages):
        for r, begin, end in stage["arrive"]:
            if begin == 0:
                wait_edges(r)
            to_next["scene", r, begin].wait_recv()
            unpack(r, begin, end, lambda i, c: base[r, i, c])
        multiply(stage)
        if n == len(stages) - 2:
            total[...] = invert(0, stage["at"] + stage["padded"])
    series = invert(stages[-1]["at"], stages[-1]["at"] + stages[-1]["padded"])
    if len(stages) > 1:
        series = series + total[...]
    for c in range(2):
        out[:, c] = series[:, c * 64:c * 64 + looks].reshape(NP, half, looks)

    for key, copy in to_next.items():
        if key[0] in ("dates", "count", "scene"):
            copy.wait_send()

    @pl.when(has_right)
    def _():
        for r in range(D):
            to_next["right", r].wait_send()

    @pl.when(has_left)
    def _():
        for r in range(D):
            to_next["left", r].wait_send()


def swapped(date, low, high):
    bit = 1
    while 2 * bit <= (low ^ high):
        bit *= 2
    return (flipped(date, low) // bit) % 2


def plan(D, A, half):
    cuts = {r: [(0, A)] for r in range(1, D)}
    cuts[D - 1] = [(0, A // 2), (A // 2, A)] if A > 1 else [(0, A)]
    stages, at = [], 0
    for r in range(1, D):
        for begin, end in cuts[r]:
            news = [(r, j) for j in range(begin, end)]
            if r == 1 and begin == 0:
                news = [(0, j) for j in range(A)] + news
            pieces, used = [], 0
            found = [(slot, j, q, A) for slot, j in news for q in range(slot)]
            found += [(slot, j, slot, j) for slot, j in news if j]
            for slot, j, q, n in found:
                pieces.append((slot, j, q, n, used))
                used += n * half
            rows = -(-used // 16) * 16
            padded = -(-used // 128) * 128
            stages.append(dict(arrive=[(r, begin, end)], pieces=pieces, used=used, rows=rows, padded=padded, at=at))
            at += padded
    return cuts, stages, at


def invert_matrix(cfg, date, dates_in, counts_in, inverse, k_high, k_low):
    D, A, R, S, NP = (cfg[k] for k in ("D", "A", "R", "S", "NP"))
    half = R // 2
    total = D * A
    codes = []
    for d in range(D):
        row = dates_in[d, 0:1, :] * total + dates_in[d, 1:2, :]
        live = iota((1, S), 1) < counts_in[d]
        codes.append(jnp.where(live, row, -1).astype(F32))
    codes.append(jnp.full((8 - D % 8 if D % 8 else 8, S), -1.0, F32))
    table = jnp.concatenate(codes, axis=0)
    table = jnp.concatenate([table, jnp.full((table.shape[0], 128 - S), -1.0, F32)], axis=1)
    turned = jnp.transpose(table)
    code = jnp.concatenate([turned[0:S, d:d + 1] for d in range(D)], axis=0).astype(jnp.int32)
    inv = inverse[...]
    spread = jnp.broadcast_to(inv[:, None, :], (NP, half, D * S)).reshape(NP * half, D * S)
    spread_high, spread_low = split(spread)
    for stage in cfg["stages"]:
        width = stage["padded"]
        place = iota((1, width), 1)
        same = (iota((NP * half, width), 0) % half) == (iota((NP * half, width), 1) % half)
        want = jnp.full((1, width), -2, jnp.int32)
        for r, j, q, n, start in stage["pieces"]:
            new, old = flipped(date, r) * A + j, flipped(date, q) * A
            swap = swapped(date, q, r) if q != r else 0
            first = swap * (new * total + old) + (1 - swap) * (old * total + new)
            step = swap + (1 - swap) * total
            inside = (place >= start) & (place < start + n * half)
            want = jnp.where(inside, first + step * ((place - start) // half), want)
        hit = jnp.where(code == want, 1.0, 0.0).astype(BF16)
        value = jnp.dot(spread_high, hit, preferred_element_type=F32) + jnp.dot(spread_low, hit, preferred_element_type=F32)
        value = jnp.where(same, value, 0.0)
        columns = slice(stage["at"], stage["at"] + width)
        k_high[:, columns], k_low[:, columns] = split(value)


def padded(cells, sides, width):
    for axis, dim in sides:
        count = lax.axis_size(axis)
        ends = count - 1
        head = lax.slice_in_dim(cells, 0, width, axis=dim)
        tail = lax.slice_in_dim(cells, cells.shape[dim] - width, cells.shape[dim], axis=dim)
        cells = jnp.concatenate(
            [
                lax.ppermute(tail, axis, [(i, (i + 1) % count) for i in range(ends)]),
                cells,
                lax.ppermute(head, axis, [((i + 1) % count, i) for i in range(ends)]),
            ],
            axis=dim,
        )
    return cells


def look_matrix(padded_width, looks_here):
    column = jnp.arange(padded_width, dtype=jnp.int32)[:, None]
    target = jnp.arange(looks_here, dtype=jnp.int32)[None, :]
    offset = (column - 8 * target).astype(jnp.float32)
    inside = (offset >= 0.0) & (offset < 16.0)
    return jnp.where(inside, (8.0 - jnp.abs(offset - 7.5)) / 64.0, 0.0)


def plain_device(scenes, pair_dates, pair_count, inverse):
    slot_count = pair_dates.shape[0]
    looks_here = scenes.shape[3] // 8
    base = lax.all_to_all(scenes, "date", split_axis=2, concat_axis=0, tiled=True)
    used_dates, used_counts = (
        lax.all_gather(pair_dates, "date", axis=0, tiled=True),
        lax.all_gather(pair_count, "date", axis=0, tiled=True),
    )
    slot_index = jnp.arange(used_dates.shape[0], dtype=jnp.int32)
    living = (slot_index % slot_count < jnp.take(used_counts, slot_index // slot_count)).astype(
        jnp.float32
    )
    primary = jnp.take(base, used_dates[:, 0], axis=0)
    secondary = jnp.take(base, used_dates[:, 1], axis=0)
    p_real = primary[:, 0].astype(jnp.float32)
    p_imag = primary[:, 1].astype(jnp.float32)
    s_real = secondary[:, 0].astype(jnp.float32)
    s_imag = secondary[:, 1].astype(jnp.float32)
    real_part = p_real * s_real + p_imag * s_imag
    imaginary = p_imag * s_real - p_real * s_imag
    products = jnp.stack([real_part, imaginary], axis=1) * living[:, None, None, None]
    products = padded(products, (("col", 3),), 4)
    pair_total = products.shape[0]
    padded_width = products.shape[3]
    half_rows = products.shape[2] // 2
    halved = products.reshape(pair_total, 2, half_rows, 2, padded_width).sum(axis=3) * 0.5
    looked = jnp.dot(
        halved.reshape(-1, padded_width),
        look_matrix(padded_width, looks_here),
        precision=lax.Precision.HIGHEST,
        preferred_element_type=jnp.float32,
    )
    looked = looked.reshape(pair_total, 2, half_rows, looks_here)
    return jnp.einsum("qk,kcrm->qcrm", inverse, looked, precision=lax.Precision.HIGHEST)


def per_device(scenes, pair_dates, pair_count, inverse):
    D, C = lax.axis_size("date"), lax.axis_size("col")
    A, _, rows, X = scenes.shape
    S, NP = pair_dates.shape[0], inverse.shape[0]
    R = rows // D
    half = R // 2
    fits = R % 16 == 0 and X % 128 == 0 and X // 8 <= 64 and D & (D - 1) == 0 and 1 < D <= 8
    fits = fits and S % 8 == 0 and S <= 128 and 16 * A <= 128
    if not fits:
        return plain_device(scenes, pair_dates, pair_count, inverse)
    cuts, stages, total = plan(D, A, half)
    cfg = dict(D=D, C=C, A=A, R=R, X=X, S=S, NP=NP, order_in=list(range(1, D)), cuts=cuts, stages=stages)
    TT = X // 128 + 1
    dma = pltpu.SemaphoreType.DMA
    vmem = pl.BlockSpec(memory_space=pltpu.VMEM)
    return pl.pallas_call(
        functools.partial(stack_kernel, cfg),
        out_shape=pltpu.VMEM((NP, 2, half, X // 8), F32),
        in_specs=[pl.BlockSpec(memory_space=pltpu.HBM)] * 4,
        out_specs=vmem,
        scratch_shapes=[
            pltpu.VMEM(scenes.shape, BF16),
            pltpu.VMEM((D, A, 2, R, X), BF16),
            pltpu.VMEM((D, 2, S), jnp.int32),
            pltpu.VMEM((D, 1, 1), jnp.int32),
            pltpu.VMEM((2, rows, 128), BF16),
            pltpu.VMEM((2, D, R, 128), BF16),
            pltpu.VMEM((2 * TT * A * R, 128), F32),
            pltpu.VMEM((2, 2 * TT, D * A, half, 128), F32),
            pltpu.VMEM((NP * half, 128), F32),
            pltpu.VMEM((total, 2 * TT * 128), BF16),
            pltpu.VMEM((total, 2 * TT * 128), BF16),
            pltpu.VMEM((2 * TT * 128, 128), BF16),
            pltpu.VMEM((NP * half, total), BF16),
            pltpu.VMEM((NP * half, total), BF16),
            pltpu.VMEM((total, 128), BF16),
            pltpu.VMEM((total, 128), BF16),
            dma, dma((D, A)), dma((D, A)), dma((D,)), dma((D,)), dma((D,)), dma((D,)), dma((2, D)), dma((2, D)),
            pltpu.VMEM(inverse.shape, F32), dma((3,)),
            pltpu.VMEM((max(stage["padded"] for stage in stages), 128), F32),
        ],
        compiler_params=pltpu.CompilerParams(collective_id=0, has_side_effects=True),
    )(scenes, pair_dates.T, pair_count.reshape(1, 1), inverse)


def solution(mesh):
    placed = (P("date", None, "groups", "col"), P("date", None), P("date"), P())
    return jax.shard_map(
        per_device,
        mesh=mesh,
        in_specs=placed,
        out_specs=P(None, None, ("groups", "date"), "col"),
        check_vma=False,
    )
```

```python
import functools

import jax
import jax.numpy as jnp
from jax import lax
from jax.experimental import pallas as pl
from jax.experimental.pallas import tpu as pltpu
from jax.sharding import PartitionSpec as P

MESH = pl.DeviceIdType.MESH
F32 = jnp.float32
BF16 = jnp.bfloat16
EDGE = 4


def flipped(place, slot):
    bit = 1
    out = place
    while bit <= slot:
        if slot & bit:
            out = out + bit - 2 * bit * ((place // bit) % 2)
        bit *= 2
    return out


def split(value):
    high = value.astype(BF16)
    return high, (value - high.astype(F32)).astype(BF16)


def iota(shape, dim):
    return lax.broadcasted_iota(jnp.int32, shape, dim)


def stack_kernel(
    cfg,
    scenes, dates, count, inverse, out,
    local, base, dates_in, counts_in, edge_out, edge_in,
    raw, cells, h_high, h_low, weights, k_high, k_low, l_high, l_low,
    load_sem, send_sem, recv_sem, dates_send, dates_recv, count_send, count_recv, edge_send, edge_recv,
    inverse_in, own_sem, early,
):
    D, C, A, R, X, S, NP = (cfg[k] for k in ("D", "C", "A", "R", "X", "S", "NP"))
    dates_total = D * A
    T = X // 128
    TT = T + 1
    half = R // 2
    looks = X // 8
    block = A * A * half
    diag = block // 2
    date = lax.axis_index("date")
    col = lax.axis_index("col")
    has_left = col > 0
    has_right = col < C - 1

    barrier = pltpu.get_barrier_semaphore()
    for r in range(1, D):
        pl.semaphore_signal(barrier, inc=1, device_id={"date": flipped(date, r)}, device_id_type=MESH)

    @pl.when(has_left)
    def _():
        for r in range(D):
            pl.semaphore_signal(barrier, inc=1, device_id={"date": flipped(date, r), "col": col - 1}, device_id_type=MESH)

    @pl.when(has_right)
    def _():
        for r in range(D):
            pl.semaphore_signal(barrier, inc=1, device_id={"date": flipped(date, r), "col": col + 1}, device_id_type=MESH)

    load = pltpu.make_async_copy(scenes, local, load_sem)
    load.start()
    own = [
        pltpu.make_async_copy(dates, dates_in.at[date], own_sem.at[0]),
        pltpu.make_async_copy(count, counts_in.at[date], own_sem.at[1]),
        pltpu.make_async_copy(inverse, inverse_in, own_sem.at[2]),
    ]

    for copy in own:
        copy.start()

    load.wait()
    lane = iota((D * R, 128), 1)
    to_left = jnp.zeros((D * R, 128), F32)
    to_right = jnp.zeros((D * R, 128), F32)
    for i in range(2 * A):
        first = local[i // 2, i % 2, :, 0:128].astype(F32)
        last = local[i // 2, i % 2, :, X - 128:X].astype(F32)
        shift = (8 * i + EDGE) % 128
        to_left = jnp.where(lane // EDGE == 2 * i + 1, pltpu.roll(first, shift, 1), to_left)
        shift = (8 * i + EDGE) % 128
        to_right = jnp.where(lane // EDGE == 2 * i, pltpu.roll(last, shift, 1), to_right)
    edge_out[0] = to_right.astype(BF16)
    edge_out[1] = to_left.astype(BF16)

    @pl.when(jnp.logical_not(has_left))
    def _():
        edge_in[0] = jnp.zeros((D, R, 128), BF16)

    @pl.when(jnp.logical_not(has_right))
    def _():
        edge_in[1] = jnp.zeros((D, R, 128), BF16)

    pl.semaphore_wait(barrier, D - 1 + D * (has_left.astype(jnp.int32) + has_right.astype(jnp.int32)))

    def rows_of(place):
        return pl.ds(pl.multiple_of(place * R, R), R)

    def remote(src, dst, ssem, rsem, device):
        return pltpu.make_async_remote_copy(src_ref=src, dst_ref=dst, send_sem=ssem, recv_sem=rsem, device_id=device, device_id_type=MESH)

    to_next = {}
    order = list(range(D - 1, 0, -1))
    for r in range(1, D):
        there = flipped(date, r)
        to_next["dates", r] = remote(dates, dates_in.at[date], dates_send.at[r], dates_recv.at[r], {"date": there})
        to_next["count", r] = remote(count, counts_in.at[date], count_send.at[r], count_recv.at[r], {"date": there})
        to_next["scene", r] = remote(scenes.at[:, :, rows_of(there), :], base.at[r], send_sem.at[r], recv_sem.at[r], {"date": there})
    for r in range(D):
        there = flipped(date, r)
        to_next["right", r] = remote(edge_out.at[0, rows_of(there)], edge_in.at[0, r], edge_send.at[0, r], edge_recv.at[0, r], {"date": there, "col": col + 1})
        to_next["left", r] = remote(edge_out.at[1, rows_of(there)], edge_in.at[1, r], edge_send.at[1, r], edge_recv.at[1, r], {"date": there, "col": col - 1})
    for r in order:
        to_next["dates", r].start()
        to_next["count", r].start()

    @pl.when(has_right)
    def _():
        for r in order + [0]:
            to_next["right", r].start()

    @pl.when(has_left)
    def _():
        for r in order + [0]:
            to_next["left", r].start()

    for r in cfg["send_order"]:
        to_next["scene", r].start()

    row = iota((TT * 128, 128), 0)
    spot = row - TT * 128 + 128
    column = jnp.where(spot < 0, row, jnp.where(spot < EDGE, spot - EDGE, spot - EDGE + X))
    usable = (spot < 2 * EDGE)
    target = iota((TT * 128, 128), 1)
    for c in range(2):
        look = target - 64 * c
        offset = column - 8 * look + 4
        inside = usable & (look >= 0) & (look < looks) & (offset >= 0) & (offset < 16)
        value = jnp.where(inside, (8.0 - jnp.abs(offset.astype(F32) - 7.5)) / 128.0, 0.0)
        weights[c * TT * 128:(c + 1) * TT * 128, :] = value.astype(BF16)

    def unpack(slot, main):
        for c in range(2):
            for t in range(T):
                for i in range(A):
                    at = ((c * TT + t) * A + i) * R
                    raw[at:at + R, :] = main(i, c)[:, t * 128:(t + 1) * 128].astype(F32)
        edges = edge_in[0, slot].astype(F32) + edge_in[1, slot].astype(F32)
        for c in range(2):
            for i in range(A):
                at = ((c * TT + T) * A + i) * R
                shift = (128 - 8 * (2 * i + c)) % 128
                raw[at:at + R, :] = pltpu.roll(edges, shift, 1) if shift else edges
        total = 2 * TT * A * half
        for parity in range(2):
            got = raw[pl.ds(parity, total, stride=2), :]
            cells[parity, :, slot * A:(slot + 1) * A] = got.reshape(2 * TT, A, half, 128)

    def emit(at, pieces):
        rows = pieces[0][0].shape[0]
        for t, both in enumerate(pieces):
            for c in range(2):
                high, low = split(both[c])
                h_high[at:at + rows, (c * TT + t) * 128:(c * TT + t + 1) * 128] = high
                h_low[at:at + rows, (c * TT + t) * 128:(c * TT + t + 1) * 128] = low

    def product(p_of, s_of, t):
        real = imaginary = None
        for parity in range(2):
            p0, p1 = p_of(parity, t), p_of(parity, TT + t)
            s0, s1 = s_of(parity, t), s_of(parity, TT + t)
            one = p0 * s0 + p1 * s1
            two = p1 * s0 - p0 * s1
            real = one if real is None else real + one
            imaginary = two if imaginary is None else imaginary + two
        return real, imaginary

    def pair_order(ra, rb):
        bit = 1
        while 2 * bit <= (ra ^ rb):
            bit *= 2
        swap = (flipped(date, ra) // bit) % 2
        low = ra + swap * (rb - ra)
        high = rb - swap * (rb - ra)
        return low, high

    chunks = []

    def cross(ra, rb):
        at = len(chunks) * block
        chunks.append((ra, rb))
        low, high = pair_order(ra, rb)
        for i in range(A):
            pieces = []
            for t in range(TT):
                both = product(
                    lambda q, n: cells[q, n, low * A + i][None],
                    lambda q, n: cells[q, n, pl.ds(high * A, A)], t)
                pieces.append([v.reshape(A * half, 128) for v in both])
            emit(at + i * A * half, pieces)

    def within(ra):
        at = len(chunks) * block
        chunks.append((ra, ra + 1))
        for side in range(2):
            slot = ra + side
            pieces = []
            for t in range(TT):
                parts = [], []
                for step in range(1, A):
                    both = product(
                        lambda q, n: cells[q, n, slot * A:slot * A + A - step],
                        lambda q, n: cells[q, n, slot * A + step:slot * A + A], t)
                    for c in range(2):
                        parts[c].append(both[c].reshape((A - step) * half, 128))
                pad = jnp.zeros((diag - A * (A - 1) // 2 * half, 128), F32)
                pieces.append([jnp.concatenate(parts[c] + [pad], axis=0) for c in range(2)])
            emit(at + side * diag, pieces)

    def look(start, stop):
        rows = slice(start * block, stop * block)
        got = jnp.dot(h_high[rows, :], weights[...], preferred_element_type=F32)
        got = got + jnp.dot(h_low[rows, :], weights[...], preferred_element_type=F32)
        l_high[rows, :], l_low[rows, :] = split(got)

    def wait_edges(r):
        @pl.when(has_left)
        def _():
            to_next["right", r].wait_recv()

        @pl.when(has_right)
        def _():
            to_next["left", r].wait_recv()

    wait_edges(0)
    unpack(0, lambda i, c: local[i, c, rows_of(date), :])

    def invert(start, stop):
        rows = slice(start * block, stop * block)
        lh, ll = l_high[rows, :], l_low[rows, :]
        kh = k_high[:, rows]
        part = jnp.dot(kh, lh, preferred_element_type=F32)
        part = part + jnp.dot(kh, ll, preferred_element_type=F32)
        return part + jnp.dot(k_low[:, rows], lh, preferred_element_type=F32)

    order_in = cfg["order_in"]
    looked = 0
    split_at = 0
    arrived = [0]
    for r in order_in:
        if r == order_in[0]:
            for copy in own:
                copy.wait()
            for q in range(1, D):
                to_next["dates", q].wait_recv()
                to_next["count", q].wait_recv()
        if r == order_in[-1]:
            split_at = looked
            early[...] = invert(0, looked) if looked else jnp.zeros(early.shape, F32)
        wait_edges(r)
        to_next["scene", r].wait_recv()
        unpack(r, lambda i, c: base[r, i, c])
        if (r ^ 1) in arrived:
            within(r & ~1)
        for other in arrived:
            cross(min(other, r), max(other, r))
        arrived.append(r)
        look(looked, len(chunks))
        looked = len(chunks)
        if r == order_in[0]:
            invert_matrix(cfg, date, dates_in, counts_in, inverse_in, k_high, k_low, pair_order)

    series = early[...] + invert(split_at, len(chunks))
    for c in range(2):
        out[:, c] = series[:, c * 64:c * 64 + looks].reshape(NP, half, looks)

    for r in range(1, D):
        for kind in ("dates", "count", "scene"):
            to_next[kind, r].wait_send()

    @pl.when(has_right)
    def _():
        for r in range(D):
            to_next["right", r].wait_send()

    @pl.when(has_left)
    def _():
        for r in range(D):
            to_next["left", r].wait_send()


def chunk_list(order_in):
    chunks, arrived = [], [0]
    for r in order_in:
        if (r ^ 1) in arrived:
            chunks.append((r & ~1, None))
        for other in arrived:
            chunks.append((min(other, r), max(other, r)))
        arrived.append(r)
    return chunks


def invert_matrix(cfg, date, dates_in, counts_in, inverse, k_high, k_low, pair_order):
    D, A, R, S, NP = (cfg[k] for k in ("D", "A", "R", "S", "NP"))
    half = R // 2
    block = A * A * half
    diag = block // 2
    total = D * A
    codes = []
    for d in range(D):
        row = dates_in[d, 0:1, :] * total + dates_in[d, 1:2, :]
        live = iota((1, S), 1) < counts_in[d]
        codes.append(jnp.where(live, row, -1).astype(F32))
    codes.append(jnp.full((8 - D % 8 if D % 8 else 8, S), -1.0, F32))
    table = jnp.concatenate(codes, axis=0)
    table = jnp.concatenate([table, jnp.full((table.shape[0], 128 - S), -1.0, F32)], axis=1)
    turned = jnp.transpose(table)
    code = jnp.concatenate([turned[0:S, d:d + 1] for d in range(D)], axis=0).astype(jnp.int32)
    inv = inverse[...]
    spread = jnp.broadcast_to(inv[:, None, :], (NP, half, D * S)).reshape(NP * half, D * S)
    spread_high, spread_low = split(spread)
    place = iota((1, block), 1)
    same = (iota((NP * half, block), 0) % half) == (iota((NP * half, block), 1) % half)
    for n, (ra, rb) in enumerate(chunk_list(cfg["order_in"])):
        if rb is None:
            slot = place // diag
            index = (place % diag) // half
            first = jnp.zeros_like(place)
            second = jnp.zeros_like(place) - 1
            at = 0
            for step in range(1, A):
                for i in range(A - step):
                    first = jnp.where(index == at, i, first)
                    second = jnp.where(index == at, i + step, second)
                    at += 1
            owner = jnp.where(slot == 0, flipped(date, ra), flipped(date, ra + 1))
            want = jnp.where(second >= 0, (owner * A + first) * total + owner * A + second, -2)
        else:
            low, high = pair_order(ra, rb)
            lo_date, hi_date = cfg["place_of"](date, low), cfg["place_of"](date, high)
            first = lo_date * A + place // (A * half)
            second = hi_date * A + (place // half) % A
            want = first * total + second
        hit = jnp.where(code == want, 1.0, 0.0).astype(BF16)
        value = jnp.dot(spread_high, hit, preferred_element_type=F32) + jnp.dot(spread_low, hit, preferred_element_type=F32)
        value = jnp.where(same, value, 0.0)
        columns = slice(n * block, (n + 1) * block)
        k_high[:, columns], k_low[:, columns] = split(value)


def padded(cells, sides, width):
    for axis, dim in sides:
        count = lax.axis_size(axis)
        ends = count - 1
        head = lax.slice_in_dim(cells, 0, width, axis=dim)
        tail = lax.slice_in_dim(cells, cells.shape[dim] - width, cells.shape[dim], axis=dim)
        cells = jnp.concatenate(
            [
                lax.ppermute(tail, axis, [(i, (i + 1) % count) for i in range(ends)]),
                cells,
                lax.ppermute(head, axis, [((i + 1) % count, i) for i in range(ends)]),
            ],
            axis=dim,
        )
    return cells


def look_matrix(padded_width, looks_here):
    column = jnp.arange(padded_width, dtype=jnp.int32)[:, None]
    target = jnp.arange(looks_here, dtype=jnp.int32)[None, :]
    offset = (column - 8 * target).astype(jnp.float32)
    inside = (offset >= 0.0) & (offset < 16.0)
    return jnp.where(inside, (8.0 - jnp.abs(offset - 7.5)) / 64.0, 0.0)


def plain_device(scenes, pair_dates, pair_count, inverse):
    slot_count = pair_dates.shape[0]
    looks_here = scenes.shape[3] // 8
    base = lax.all_to_all(scenes, "date", split_axis=2, concat_axis=0, tiled=True)
    used_dates, used_counts = (
        lax.all_gather(pair_dates, "date", axis=0, tiled=True),
        lax.all_gather(pair_count, "date", axis=0, tiled=True),
    )
    slot_index = jnp.arange(used_dates.shape[0], dtype=jnp.int32)
    living = (slot_index % slot_count < jnp.take(used_counts, slot_index // slot_count)).astype(
        jnp.float32
    )
    primary = jnp.take(base, used_dates[:, 0], axis=0)
    secondary = jnp.take(base, used_dates[:, 1], axis=0)
    p_real = primary[:, 0].astype(jnp.float32)
    p_imag = primary[:, 1].astype(jnp.float32)
    s_real = secondary[:, 0].astype(jnp.float32)
    s_imag = secondary[:, 1].astype(jnp.float32)
    real_part = p_real * s_real + p_imag * s_imag
    imaginary = p_imag * s_real - p_real * s_imag
    products = jnp.stack([real_part, imaginary], axis=1) * living[:, None, None, None]
    products = padded(products, (("col", 3),), 4)
    pair_total = products.shape[0]
    padded_width = products.shape[3]
    half_rows = products.shape[2] // 2
    halved = products.reshape(pair_total, 2, half_rows, 2, padded_width).sum(axis=3) * 0.5
    looked = jnp.dot(
        halved.reshape(-1, padded_width),
        look_matrix(padded_width, looks_here),
        precision=lax.Precision.HIGHEST,
        preferred_element_type=jnp.float32,
    )
    looked = looked.reshape(pair_total, 2, half_rows, looks_here)
    return jnp.einsum("qk,kcrm->qcrm", inverse, looked, precision=lax.Precision.HIGHEST)


def per_device(scenes, pair_dates, pair_count, inverse):
    D, C = lax.axis_size("date"), lax.axis_size("col")
    A, _, rows, X = scenes.shape
    S, NP = pair_dates.shape[0], inverse.shape[0]
    R = rows // D
    half = R // 2
    block = A * A * half
    fits = R % 16 == 0 and X % 128 == 0 and X // 8 <= 64 and D & (D - 1) == 0 and 1 < D and S % 8 == 0 and S <= 128
    fits = fits and block % 128 == 0 and A * (A - 1) // 2 * half <= block // 2 and (block // 2) % 16 == 0 and 8 * 2 * A <= 128
    if not fits or D > 8:
        return plain_device(scenes, pair_dates, pair_count, inverse)
    order_in = list(range(1, D))
    cfg = dict(D=D, C=C, A=A, R=R, X=X, S=S, NP=NP, order_in=order_in, send_order=order_in, place_of=place_of(D))
    total = len(chunk_list(order_in)) * block
    TT = X // 128 + 1
    dma = pltpu.SemaphoreType.DMA
    vmem = pl.BlockSpec(memory_space=pltpu.VMEM)
    return pl.pallas_call(
        functools.partial(stack_kernel, cfg),
        out_shape=pltpu.VMEM((NP, 2, half, X // 8), F32),
        in_specs=[pl.BlockSpec(memory_space=pltpu.HBM)] * 4,
        out_specs=vmem,
        scratch_shapes=[
            pltpu.VMEM(scenes.shape, BF16),
            pltpu.VMEM((D, A, 2, R, X), BF16),
            pltpu.VMEM((D, 2, S), jnp.int32),
            pltpu.VMEM((D, 1, 1), jnp.int32),
            pltpu.VMEM((2, rows, 128), BF16),
            pltpu.VMEM((2, D, R, 128), BF16),
            pltpu.VMEM((2 * TT * A * R, 128), F32),
            pltpu.VMEM((2, 2 * TT, D * A, half, 128), F32),
            pltpu.VMEM((total, 2 * TT * 128), BF16),
            pltpu.VMEM((total, 2 * TT * 128), BF16),
            pltpu.VMEM((2 * TT * 128, 128), BF16),
            pltpu.VMEM((NP * half, total), BF16),
            pltpu.VMEM((NP * half, total), BF16),
            pltpu.VMEM((total, 128), BF16),
            pltpu.VMEM((total, 128), BF16),
            dma, dma((D,)), dma((D,)), dma((D,)), dma((D,)), dma((D,)), dma((D,)), dma((2, D)), dma((2, D)),
            pltpu.VMEM(inverse.shape, F32), dma((3,)), pltpu.VMEM((NP * half, 128), F32),
        ],
        compiler_params=pltpu.CompilerParams(collective_id=0, has_side_effects=True),
    )(scenes, pair_dates.T, pair_count.reshape(1, 1), inverse)


def place_of(D):
    def combine(place, slot):
        out, bit = 0, 1
        while bit < D:
            a, b = (place // bit) % 2, (slot // bit) % 2
            out = out + bit * (a + b - 2 * a * b)
            bit *= 2
        return out
    return combine


def solution(mesh):
    placed = (P("date", None, "groups", "col"), P("date", None), P("date"), P())
    return jax.shard_map(
        per_device,
        mesh=mesh,
        in_specs=placed,
        out_specs=P(None, None, ("groups", "date"), "col"),
        check_vma=False,
    )
```
